32 devices in a mesh: shard: 4 (over z), ctx: 4 (over x, core), tp: 2 (over y).
Axes of the slice: x: 2, y: 2, z: 4, core: 2. Of those that a mesh axis runs over, the one named last changes fastest.
Arguments:
- tokens: bfloat16 [12288, 2048], P(('shard', 'ctx')), may hold values from -6 to 6
- seg_ids: int32 [12288], P('shard'), may hold values from 0 to 4, as said below
- positions: int32 [12288], P('shard'), may hold values from 0 to 3068, as said below
- cotangent: bfloat16 [12288, 2048], P(('shard', 'ctx')), may hold values from -6 to 6
- norm_in: bfloat16 [2048], P(('shard', 'ctx')), may hold values from 0.5 to 1.5
- norm_mid: bfloat16 [2048], P(('shard', 'ctx')), may hold values from 0.5 to 1.5
- query_gain: bfloat16 [128], P(('shard', 'ctx')), may hold values from 0.8984375 to 1.5
- key_gain: bfloat16 [128], P(('shard', 'ctx')), may hold values from 0.8984375 to 1.5
- query_weight: bfloat16 [2048, 2048], P(('shard', 'ctx'), 'tp'), may hold values from -0.125 to 0.125
- key_matrix: bfloat16 [2048, 1024], P(('shard', 'ctx'), 'tp'), may hold values from -0.125 to 0.125
- value_matrix: bfloat16 [2048, 1024], P(('shard', 'ctx'), 'tp'), may hold values from -0.125 to 0.125
- head_weight: bfloat16 [2048, 16], P(('shard', 'ctx'), 'tp'), may hold values from -0.125 to 0.125
- out_weight: bfloat16 [2048, 2048], P('tp', ('shard', 'ctx')), may hold values from -3 to 3
- gate_weight: bfloat16 [2048, 6144], P(('shard', 'ctx'), 'tp'), may hold values from -0.125 to 0.125
- up_weight: bfloat16 [2048, 6144], P(('shard', 'ctx'), 'tp'), may hold values from -0.125 to 0.125
- down_weight: bfloat16 [6144, 2048], P('tp', ('shard', 'ctx')), may hold values from -0.078125 to 0.078125
Outputs:
- output: bfloat16 [12288, 2048], P(('shard', 'ctx'))
- input_grad: float32 [12288, 2048], P(('shard', 'ctx'))
- grad_norm_in: float32 [2048], P(('shard', 'ctx'))
- grad_norm_mid: float32 [2048], P(('shard', 'ctx'))
- grad_query_gain: float32 [128], P(('shard', 'ctx'))
- grad_key_gain: float32 [128], P(('shard', 'ctx'))
- grad_query: float32 [2048, 2048], P(('shard', 'ctx'), 'tp')
- grad_key: float32 [2048, 1024], P(('shard', 'ctx'), 'tp')
- grad_value: float32 [2048, 1024], P(('shard', 'ctx'), 'tp')
- grad_head: float32 [2048, 16], P(('shard', 'ctx'), 'tp')
- grad_out: float32 [2048, 2048], P('tp', ('shard', 'ctx'))
- grad_gate: float32 [2048, 6144], P(('shard', 'ctx'), 'tp')
- grad_up: float32 [2048, 6144], P(('shard', 'ctx'), 'tp')
- grad_down: float32 [6144, 2048], P('tp', ('shard', 'ctx'))
The draws below stay inside these ranges and needn't reach their ends.
Inputs may be any that keep to these rules, and one draw needn't show every extreme that they name: `seg_ids`: in each group's blocks of 768 rows the first 512 rows have segment 0 and the others hold, block after block, a stream of 1024 rows in which continuations 1 to 4 follow in order, each one row or more. Prompt rows of a group have positions 0, 1, ... in the order of the blocks; the rows of a continuation have 2048, 2049, ... in stream order; in the first group continuations 1 to 3 have one row each.
All inputs are finite; a program needn't handle non-finite values.
Results may differ from the reference program's by a relative error of at most 0.014.
Values may be sent and summed in bfloat16 or wider, within the bound.
No kernel may reach another device: no remote copies, remote signals or barrier semaphores. Data moves between devices by JAX's collectives and lax.ppermute only.
A program may use at most 384 MiB of HBM per device.

```python
import jax
import jax.numpy as jnp
from jax import lax

MODEL_WIDTH = 2048
QUERY_HEADS = 16
KEY_VALUE_HEADS = 8
HEAD_SIZE = 128
FF = 6144
NCONT = 4
PD = 512
CD = 256
GROUP_COUNT = 4
PROMPT = 2048
CSTREAM = 1024
GROUP_TOKENS = 3072
TOTAL_TOKENS = 12288
N_CTX = 4


def stream_layout(key):
    base_key = jax.random.fold_in(key, 7)
    stream_index = jnp.arange(CSTREAM, dtype=jnp.int32)
    fixed_cuts = jnp.arange(1, NCONT, dtype=jnp.int32)

    def one_group(group_key, group_number):
        shuffled = jax.random.permutation(group_key, CSTREAM - 1)
        random_cuts = jnp.sort(shuffled[:NCONT - 1] + 1).astype(jnp.int32)
        cut_points = jnp.where(group_number == 0, fixed_cuts, random_cuts)
        passed = cut_points[None, :] <= stream_index[:, None]
        segment = 1 + jnp.sum(passed.astype(jnp.int32), axis=1)
        starts = jnp.max(jnp.where(passed, cut_points[None, :], 0), axis=1)
        return (segment, PROMPT + stream_index - starts)
    group_keys = jax.random.split(base_key, GROUP_COUNT)
    group_numbers = jnp.arange(GROUP_COUNT, dtype=jnp.int32)
    segment, places = jax.vmap(one_group)(group_keys, group_numbers)
    prompt_seg = jnp.zeros((GROUP_COUNT, N_CTX, PD), jnp.int32)
    prompt_pos = jnp.broadcast_to(jnp.arange(PROMPT, dtype=jnp.int32).reshape(1, N_CTX, PD), (GROUP_COUNT, N_CTX, PD))
    all_seg = jnp.concatenate([prompt_seg, segment.reshape(GROUP_COUNT, N_CTX, CD)], axis=2).reshape(TOTAL_TOKENS)
    all_pos = jnp.concatenate([prompt_pos, places.reshape(GROUP_COUNT, N_CTX, CD)], axis=2).reshape(TOTAL_TOKENS)
    return (all_seg, all_pos)


def draw_seg_ids(key, part):
    return stream_layout(key)[0]


def draw_positions(key, part):
    return stream_layout(key)[1]


def strengthened(drawn, rng, source, target, shards_of, factor):
    def block_of(position):
        return (jnp.arange(drawn.shape[position]) // (drawn.shape[position] // shards_of)).reshape((-1,) + (1,) * (drawn.ndim - 1 - position))

    near = jax.random.permutation(rng, shards_of)[block_of(target)]
    far = (block_of(target) + shards_of // 2) % shards_of
    return jnp.where((block_of(source) == near) | (block_of(source) == far), factor * drawn, drawn)


def level_of(key, shape, shards, low, largest):
    level = 1.0
    for dim, blocks in shards:
        steps = jax.random.uniform(jax.random.fold_in(jax.random.fold_in(key, 6), dim), (blocks,), jnp.float32, low / len(shards), largest / len(shards))
        level = level * jnp.repeat(jnp.exp(steps), shape[dim] // blocks).reshape((-1,) + (1,) * (len(shape) - 1 - dim))
    return level


def gaussian(stream_key, shape, scale, most, shards=(), kind=jnp.bfloat16):
    values = jax.random.normal(stream_key, shape, jnp.float32) * scale
    if len(shards) > 0:
        values = level_of(stream_key, shape, shards, -0.22, 0.18) * values
    return jnp.clip(values, min=-most, max=most).astype(kind)


def gaussian_with(stream_key, extent, deviation, most, pieces, heavy, kind=jnp.bfloat16):
    values = deviation * jax.random.normal(stream_key, extent, jnp.float32)
    if pieces:
        values = values * level_of(stream_key, extent, pieces, -0.22, 0.18)
    return jnp.clip(strengthened(values, jax.random.fold_in(stream_key, 3), *heavy), -most, most).astype(kind)


def setup_inputs(seed: int = 0) -> dict:
    splits = jax.random.split(jax.random.key(seed), 17)
    tokens = gaussian_with(splits[0], (TOTAL_TOKENS, MODEL_WIDTH), 1.0, 6.0, ((0, 16),), (0, 1, 16, 2.0))
    seg_ids = draw_seg_ids(jax.random.fold_in(splits[16], 71), 0)
    positions = draw_positions(jax.random.fold_in(splits[16], 71), 0)
    cotangent = gaussian_with(splits[3], (TOTAL_TOKENS, MODEL_WIDTH), 1.0, 6.0, ((0, 16),), (0, 1, 16, 2.0))
    norm_in = jnp.clip(1.0 + 0.1 * jax.random.normal(splits[4], (MODEL_WIDTH,), jnp.float32), 0.5, 1.5).astype(jnp.bfloat16)
    norm_mid = jnp.clip(1.0 + 0.1 * jax.random.normal(splits[5], (MODEL_WIDTH,), jnp.float32), 0.5, 1.5).astype(jnp.bfloat16)
    query_gain = jnp.clip(0.8984375 + 0.6015625 * jax.random.uniform(splits[6], (HEAD_SIZE,), jnp.float32) ** level_of(splits[6], (HEAD_SIZE,), ((0, 16),), -0.2, 0.2), 0.8984375, 1.5).astype(jnp.bfloat16)
    key_gain = jnp.clip(0.8984375 + 0.6015625 * jax.random.uniform(splits[7], (HEAD_SIZE,), jnp.float32) ** level_of(splits[7], (HEAD_SIZE,), ((0, 16),), -0.2, 0.2), 0.8984375, 1.5).astype(jnp.bfloat16)
    query_weight = gaussian(splits[8], (MODEL_WIDTH, QUERY_HEADS * HEAD_SIZE), MODEL_WIDTH ** -0.5, 0.125, ((0, 16), (1, 2)))
    key_matrix = gaussian(splits[9], (MODEL_WIDTH, KEY_VALUE_HEADS * HEAD_SIZE), MODEL_WIDTH ** -0.5, 0.125, ((0, 16), (1, 2)))
    value_matrix = gaussian(splits[10], (MODEL_WIDTH, KEY_VALUE_HEADS * HEAD_SIZE), MODEL_WIDTH ** -0.5, 0.125, ((0, 16), (1, 2)))
    head_weight = gaussian(splits[11], (MODEL_WIDTH, QUERY_HEADS), MODEL_WIDTH ** -0.5, 0.125, ((0, 16), (1, 2)))
    out_weight = gaussian(splits[12], (QUERY_HEADS * HEAD_SIZE, MODEL_WIDTH), (max(QUERY_HEADS * HEAD_SIZE // 512, 1)) ** -0.5, 3.0, ((0, 2), (1, 16)))
    gate_weight = gaussian(splits[13], (MODEL_WIDTH, FF), MODEL_WIDTH ** -0.5, 0.125, ((0, 16), (1, 2)))
    up_weight = gaussian(splits[14], (MODEL_WIDTH, FF), MODEL_WIDTH ** -0.5, 0.125, ((0, 16), (1, 2)))
    down_weight = gaussian(splits[15], (FF, MODEL_WIDTH), FF ** -0.5, 0.078125, ((0, 2), (1, 16)))
    return {"tokens": tokens, "seg_ids": seg_ids, "positions": positions, "cotangent": cotangent, "norm_in": norm_in, "norm_mid": norm_mid, "query_gain": query_gain, "key_gain": key_gain, "query_weight": query_weight, "key_matrix": key_matrix, "value_matrix": value_matrix, "head_weight": head_weight, "out_weight": out_weight, "gate_weight": gate_weight, "up_weight": up_weight, "down_weight": down_weight}


EPS = 1e-06
THETA = 1000000.0
HIGH_PRECISION = lax.Precision.HIGHEST

@jax.custom_vjp
def reduced_precision(v):
    return lax.optimization_barrier(v.astype(jnp.bfloat16)).astype(jnp.float32)

@jax.custom_vjp
def reduced_backward(v):
    return v

def low_keep(v):
    return (reduced_precision(v), None)

def low_pass(kept, grad):
    return (grad,)

def back_keep(v):
    return (v, None)

def back_low(kept, grad):
    return (reduced_precision(grad),)
reduced_precision.defvjp(low_keep, low_pass)
reduced_backward.defvjp(back_keep, back_low)

def rms_norm(values, gain):
    scale = lax.rsqrt(lax.optimization_barrier(jnp.mean(values * values, axis=-1, keepdims=True)) + EPS)
    return values * scale * gain

def rotate(values, places):
    half_width = values.shape[-1] // 2
    frequency = THETA ** (-(jnp.arange(half_width, dtype=jnp.float32) * 2.0) / values.shape[-1])
    angles = places.astype(jnp.float32)[:, None] * frequency[None, :]
    cos_table = jnp.cos(angles)[:, None, :]
    sin_table = jnp.sin(angles)[:, None, :]
    first = values[..., :half_width]
    second = values[..., half_width:]
    return jnp.concatenate([first * cos_table - second * sin_table, second * cos_table + first * sin_table], axis=-1)

def attend_head(queries, keys, values, segments, places):
    scores = jnp.einsum('qrd,kd->rqk', queries, keys, precision=HIGH_PRECISION) * HEAD_SIZE ** (-0.5)
    scores = reduced_backward(scores)
    allowed = ((segments[None, :] == 0) | (segments[None, :] == segments[:, None])) & (places[None, :] <= places[:, None])
    scores = jnp.where(allowed[None], scores, -1e+30)
    highest = lax.optimization_barrier(jnp.max(scores, axis=-1, keepdims=True))
    weights_exp = jnp.exp(scores - highest)
    probs = weights_exp / lax.optimization_barrier(jnp.sum(weights_exp, axis=-1, keepdims=True))
    return jnp.einsum('rqk,kd->qrd', reduced_precision(probs), values, precision=HIGH_PRECISION)

def forward(tokens, norm_in, norm_mid, query_gain, key_gain, query_weight, key_matrix, value_matrix, head_weight, out_weight, gate_weight, up_weight, down_weight, seg_ids, positions):
    shared_prefix = QUERY_HEADS // KEY_VALUE_HEADS
    normalized_input = reduced_precision(rms_norm(tokens, norm_in))
    query_raw = reduced_backward(jnp.dot(normalized_input, query_weight, precision=HIGH_PRECISION)).reshape(TOTAL_TOKENS, QUERY_HEADS, HEAD_SIZE)
    key_unnormed = reduced_backward(jnp.dot(normalized_input, key_matrix, precision=HIGH_PRECISION)).reshape(TOTAL_TOKENS, KEY_VALUE_HEADS, HEAD_SIZE)
    value_reduced = reduced_precision(reduced_backward(jnp.dot(normalized_input, value_matrix, precision=HIGH_PRECISION))).reshape(TOTAL_TOKENS, KEY_VALUE_HEADS, HEAD_SIZE)
    head_logit = reduced_backward(jnp.dot(normalized_input, head_weight, precision=HIGH_PRECISION))
    query_reduced = reduced_precision(rotate(rms_norm(query_raw, query_gain), positions))
    key_reduced = reduced_precision(rotate(rms_norm(key_unnormed, key_gain), positions))
    grouped_queries = jnp.moveaxis(query_reduced.reshape(GROUP_COUNT, GROUP_TOKENS, KEY_VALUE_HEADS, shared_prefix, HEAD_SIZE), 2, 1)
    grouped_keys = jnp.moveaxis(key_reduced.reshape(GROUP_COUNT, GROUP_TOKENS, KEY_VALUE_HEADS, HEAD_SIZE), 2, 1)
    grouped_values = jnp.moveaxis(value_reduced.reshape(GROUP_COUNT, GROUP_TOKENS, KEY_VALUE_HEADS, HEAD_SIZE), 2, 1)
    seg_groups = seg_ids.reshape(GROUP_COUNT, GROUP_TOKENS)
    pos_groups = positions.reshape(GROUP_COUNT, GROUP_TOKENS)

    def one_group(carry_in, group_item):
        group_queries, group_keys, group_values, segments, places = group_item

        def one_head(head_item):
            return attend_head(head_item[0], head_item[1], head_item[2], segments, places)
        return (carry_in, lax.map(jax.checkpoint(one_head), (group_queries, group_keys, group_values)))
    carry_out, attended = lax.scan(one_group, jnp.zeros((), jnp.float32), (grouped_queries, grouped_keys, grouped_values, seg_groups, pos_groups))
    attended = reduced_backward(jnp.moveaxis(attended, 1, 2).reshape(TOTAL_TOKENS, QUERY_HEADS, HEAD_SIZE))
    gated = reduced_precision(attended * jax.nn.sigmoid(head_logit)[:, :, None]).reshape(TOTAL_TOKENS, QUERY_HEADS * HEAD_SIZE)
    middle = tokens + reduced_backward(jnp.dot(gated, out_weight, precision=HIGH_PRECISION))
    normed_mid = reduced_precision(rms_norm(middle, norm_mid))
    gate_value = reduced_backward(jnp.dot(normed_mid, gate_weight, precision=HIGH_PRECISION))
    up_value = reduced_backward(jnp.dot(normed_mid, up_weight, precision=HIGH_PRECISION))
    hidden = reduced_precision(jax.nn.silu(gate_value) * up_value)
    return middle + reduced_backward(jnp.dot(hidden, down_weight, precision=HIGH_PRECISION))

def reference(tokens, seg_ids, positions, cotangent, norm_in, norm_mid, query_gain, key_gain, query_weight, key_matrix, value_matrix, head_weight, out_weight, gate_weight, up_weight, down_weight):
    floats = [array.astype(jnp.float32) for array in (tokens, norm_in, norm_mid, query_gain, key_gain, query_weight, key_matrix, value_matrix, head_weight, out_weight, gate_weight, up_weight, down_weight)]

    def wrapped(*arrays):
        return forward(*arrays, seg_ids, positions)
    result, pullback = jax.vjp(wrapped, *floats)
    grads = pullback(cotangent.astype(jnp.float32))
    return (result.astype(jnp.bfloat16), grads[0], grads[1], grads[2], grads[3], grads[4], grads[5], grads[6], grads[7], grads[8], grads[9], grads[10], grads[11], grads[12])
```

```python
import functools
import math

import jax
import jax.numpy as jnp
import numpy as np
from jax import lax
from jax.experimental import pallas as pl
from jax.experimental.pallas import tpu as pltpu
from jax.sharding import PartitionSpec as P

HEAD = 128
LANES = 128
EPS = 1e-06
THETA = 1000000.0
MASKED = -1e30
LOG2E = 1.4426950408889634
SCALE = HEAD ** (-0.5)
KEY_TILE = 256
CHUNKS = 3

F32 = jnp.float32
BF16 = jnp.bfloat16


def matmul(a, b, dims=((1,), (0,))):
    return lax.dot_general(a, b, (dims, ((), ())), preferred_element_type=F32)


def ring_tables(n_shard, n_ctx):
    path = []
    for x in range(n_ctx // 2):
        column = range(n_shard) if x % 2 == 0 else reversed(range(n_shard))
        path += [(z, x) for z in column]
    length = len(path)

    def device(place, core):
        z, x = path[place % length]
        return z * n_ctx + x * 2 + core

    hops = [(device(r, 0), device(r + 1, 0)) for r in range(length)]
    hops += [(device(r, 1), device(r - 1, 1)) for r in range(length)]
    order = np.zeros((n_shard * n_ctx, 2 * length), np.int32)
    for r in range(length):
        for core in (0, 1):
            back = -1 if core == 0 else 1
            own = [device(r + back * s, core) for s in range(length)]
            other = [device(r - back * s, 1 - core) for s in range(length)]
            order[device(r, core)] = own + other
    return hops, order, length


RING_AXES = ("shard", "ctx")


class Ring:
    def __init__(self, n_shard, n_ctx):
        self.hops, self.order, self.length = ring_tables(n_shard, n_ctx)
        self.swaps = [(i, i ^ 1) for i in range(n_ctx)]

    def hop(self, value):
        return lax.ppermute(value, RING_AXES, self.hops)

    def swap(self, value):
        return lax.ppermute(value, "ctx", self.swaps)

    def gather(self, block):
        pieces = [block]
        for _ in range(self.length - 1):
            pieces.append(self.hop(pieces[-1]))
        return pieces

    def assemble(self, pieces):
        return jnp.concatenate(pieces + [self.swap(piece) for piece in pieces], axis=0)

    def reduce(self, kept):
        rows = kept.shape[0] // self.length
        total = kept[rows : 2 * rows]
        for step in range(2, self.length + 1):
            place = (step % self.length) * rows
            total = self.hop(total).astype(F32) + kept[place : place + rows].astype(F32)
            if step < self.length:
                total = total.astype(BF16)
        return total


def after(value, *others):
    return lax.optimization_barrier((value, *others))[0]


def tp_scatter(partial, n_tp):
    rows = partial.shape[0] // n_tp
    total = partial[:rows]
    for j in range(1, n_tp):
        sent = partial[j * rows : (j + 1) * rows].astype(BF16)
        total = total + lax.ppermute(
            sent, "tp", [(i, (i + j) % n_tp) for i in range(n_tp)]
        ).astype(F32)
    return total


def tp_gather(block, n_tp):
    blocks = [block]
    for j in range(1, n_tp):
        blocks.append(lax.ppermute(block, "tp", [(i, (i - j) % n_tp) for i in range(n_tp)]))
    return blocks


def tp_total(value, n_tp):
    total = value
    for j in range(1, n_tp):
        total = total + lax.ppermute(value, "tp", [(i, (i + j) % n_tp) for i in range(n_tp)])
    return total


def row_tile(rows):
    return next(tile for tile in (128, 96, 64, 48, 32, 16) if rows % tile == 0)


def params(mib=48):
    return pltpu.CompilerParams(vmem_limit_bytes=mib << 20)


def enter_kernel(order_ref, rows_ref, tok_ref, cot_ref, tok_out, cot_out, scale_out):
    value = tok_ref[...].astype(F32)
    scale = lax.rsqrt(jnp.mean(value * value, axis=-1, keepdims=True) + EPS)
    scale_out[...] = jnp.broadcast_to(scale, scale_out.shape)
    blocks = tok_ref.shape[1] // LANES
    for j in range(blocks):
        source = pl.multiple_of(order_ref[j] * LANES, LANES)
        here = slice(j * LANES, (j + 1) * LANES)
        tok_out[:, here] = tok_ref[:, pl.ds(source, LANES)]
        cot_out[:, here] = cot_ref[:, pl.ds(source, LANES)]


def enter(order, tiles, tile, tokens, cotangent):
    rows, width = tokens.shape
    block = pl.BlockSpec((tile, width), lambda i, order, tiles: (tiles[i], 0))
    out = pl.BlockSpec((tile, width), lambda i, order, tiles: (i, 0))
    return pl.pallas_call(
        enter_kernel,
        grid_spec=pltpu.PrefetchScalarGridSpec(
            num_scalar_prefetch=2,
            grid=(rows // tile,),
            in_specs=[block, block],
            out_specs=[
                out,
                out,
                pl.BlockSpec((tile, LANES), lambda i, order, tiles: (i, 0)),
            ],
        ),
        out_shape=[
            jax.ShapeDtypeStruct((rows, width), BF16),
            jax.ShapeDtypeStruct((rows, width), BF16),
            jax.ShapeDtypeStruct((rows, LANES), F32),
        ],
        compiler_params=params(),
        name="enter",
    )(order, tiles, tokens, cotangent)


def leave_kernel(order_ref, value_ref, out_ref):
    blocks = value_ref.shape[1] // LANES
    for j in range(blocks):
        target = pl.multiple_of(order_ref[j] * LANES, LANES)
        out_ref[:, pl.ds(target, LANES)] = value_ref[:, j * LANES : (j + 1) * LANES].astype(
            out_ref.dtype
        )


def leave(order, tiles, tile, value, dtype, name):
    rows, width = value.shape
    return pl.pallas_call(
        lambda order, tiles, value, out: leave_kernel(order, value, out),
        grid_spec=pltpu.PrefetchScalarGridSpec(
            num_scalar_prefetch=2,
            grid=(rows // tile,),
            in_specs=[pl.BlockSpec((tile, width), lambda i, order, tiles: (i, 0))],
            out_specs=pl.BlockSpec((tile, width), lambda i, order, tiles: (tiles[i], 0)),
        ),
        out_shape=jax.ShapeDtypeStruct((rows, width), dtype),
        compiler_params=params(),
        name=name,
    )(order, tiles, value)


def turn(value, cos, sin):
    return value * cos + pltpu.roll(value, HEAD // 2, 1) * sin


def heads_kernel(
    q_heads, k_heads, tiles_ref, a_ref, b_ref, cos_ref, sin_ref, qg_ref, kg_ref, q_out, kv_out, sg_out
):
    cos, sin = cos_ref[...], sin_ref[...]

    def rotated(value, gain):
        scale = lax.rsqrt(jnp.mean(value * value, axis=-1, keepdims=True) + EPS)
        return turn(value * scale * gain, cos, sin).astype(BF16)

    for h in range(q_heads):
        here = slice(h * HEAD, (h + 1) * HEAD)
        q_out[:, here] = rotated(a_ref[:, here], qg_ref[...])
    for h in range(k_heads):
        here = slice(h * HEAD, (h + 1) * HEAD)
        kv_out[:, here] = rotated(b_ref[:, here], kg_ref[...])
    kv_out[:, k_heads * HEAD :] = b_ref[:, k_heads * HEAD :].astype(BF16)
    sg_out[...] = jax.nn.sigmoid(a_ref[:, q_heads * HEAD :])


def make_heads(tiles, tile, raw_a, raw_b, cos, sin, q_gain, k_gain, q_heads, k_heads):
    rows = raw_a.shape[0]

    def at(width):
        return pl.BlockSpec((tile, width), lambda i, tiles: (i, 0))

    gain = pl.BlockSpec((1, HEAD), lambda i, tiles: (0, 0))
    return pl.pallas_call(
        functools.partial(heads_kernel, q_heads, k_heads),
        grid_spec=pltpu.PrefetchScalarGridSpec(
            num_scalar_prefetch=1,
            grid=(rows // tile,),
            in_specs=[at(raw_a.shape[1]), at(raw_b.shape[1]), at(HEAD), at(HEAD), gain, gain],
            out_specs=[
                at(q_heads * HEAD),
                pl.BlockSpec((tile, 2 * k_heads * HEAD), lambda i, tiles: (tiles[i], 0)),
                at(LANES),
            ],
        ),
        out_shape=[
            jax.ShapeDtypeStruct((rows, q_heads * HEAD), BF16),
            jax.ShapeDtypeStruct((rows, 2 * k_heads * HEAD), BF16),
            jax.ShapeDtypeStruct((rows, LANES), F32),
        ],
        compiler_params=params(),
        name="make_heads",
    )(tiles, raw_a, raw_b, cos, sin, q_gain, k_gain)


def heads_back_kernel(
    q_heads, k_heads, tiles_ref, *refs
):
    (dq_ref, dkv1_ref, dkv2_ref, dkv3_ref, dlog_ref, a_ref, b_ref, cos_ref, sin_ref, qg_ref, kg_ref) = refs[:11]
    a_out, b_out, gain_out = refs[11:]

    @pl.when(pl.program_id(0) == 0)
    def _():
        gain_out[...] = jnp.zeros_like(gain_out)

    cos, sin = cos_ref[...], -sin_ref[...]

    def back(grad, value, gain):
        scale = lax.rsqrt(jnp.mean(value * value, axis=-1, keepdims=True) + EPS)
        unit = value * scale
        turned = turn(grad, cos, sin)
        scaled = turned * gain
        result = scale * (scaled - unit * jnp.mean(scaled * unit, axis=-1, keepdims=True))
        return result.astype(BF16), jnp.sum(turned * unit, axis=0, keepdims=True)

    q_total = jnp.zeros((1, HEAD), F32)
    k_total = jnp.zeros((1, HEAD), F32)
    for h in range(q_heads):
        here = slice(h * HEAD, (h + 1) * HEAD)
        a_out[:, here], more = back(dq_ref[:, here], a_ref[:, here], qg_ref[...])
        q_total += more
    a_out[:, q_heads * HEAD :] = dlog_ref[...]

    def total(here):
        return (
            dkv1_ref[:, here].astype(F32)
            + dkv2_ref[:, here].astype(F32)
            + dkv3_ref[:, here].astype(F32)
        )

    for h in range(k_heads):
        here = slice(h * HEAD, (h + 1) * HEAD)
        b_out[:, here], more = back(total(here), b_ref[:, here], kg_ref[...])
        k_total += more
    there = slice(k_heads * HEAD, 2 * k_heads * HEAD)
    b_out[:, there] = total(there).astype(BF16)
    gain_out[0:1, :] += q_total
    gain_out[1:2, :] += k_total


def heads_back(tiles, tile, dq, dkvs, dlog, raw_a, raw_b, cos, sin, q_gain, k_gain, q_heads, k_heads):
    rows = raw_a.shape[0]

    def at(width):
        return pl.BlockSpec((tile, width), lambda i, tiles: (i, 0))

    gain = pl.BlockSpec((1, HEAD), lambda i, tiles: (0, 0))
    moved = pl.BlockSpec((tile, 2 * k_heads * HEAD), lambda i, tiles: (tiles[i], 0))
    return pl.pallas_call(
        functools.partial(heads_back_kernel, q_heads, k_heads),
        grid_spec=pltpu.PrefetchScalarGridSpec(
            num_scalar_prefetch=1,
            grid=(rows // tile,),
            in_specs=[
                at(q_heads * HEAD),
                moved,
                moved,
                moved,
                at(LANES),
                at(raw_a.shape[1]),
                at(raw_b.shape[1]),
                at(HEAD),
                at(HEAD),
                gain,
                gain,
            ],
            out_specs=[
                at(raw_a.shape[1]),
                at(raw_b.shape[1]),
                pl.BlockSpec((8, HEAD), lambda i, tiles: (0, 0)),
            ],
        ),
        out_shape=[
            jax.ShapeDtypeStruct(raw_a.shape, BF16),
            jax.ShapeDtypeStruct(raw_b.shape, BF16),
            jax.ShapeDtypeStruct((8, HEAD), F32),
        ],
        compiler_params=params(),
        name="heads_back",
    )(tiles, dq, *dkvs, dlog, raw_a, raw_b, cos, sin, q_gain, k_gain)


def load_keys(kv_refs, kv_all, sem, block_rows):
    copies = [
        pltpu.make_async_copy(ref, kv_all.at[pl.ds(m * block_rows, block_rows)], sem.at[m])
        for m, ref in enumerate(kv_refs)
    ]
    for copy in copies:
        copy.start()
    for copy in copies:
        copy.wait()


def stacked(ref, g, share):
    return jnp.concatenate(
        [ref[:, (g * share + j) * HEAD : (g * share + j + 1) * HEAD] for j in range(share)], axis=0
    )


def attend_kernel(q_heads, k_heads, blocks, flags_ref, *refs):
    q_ref, bias_ref, sg_ref = refs[:3]
    kv_refs = refs[3 : 3 + blocks]
    att_out, gated_out, lse_out = refs[3 + blocks : 6 + blocks]
    kv_all, acc, norm, sem = refs[6 + blocks :]
    share = q_heads // k_heads
    tile = q_ref.shape[0]
    step = pl.program_id(0)
    key_tiles = kv_all.shape[0] // KEY_TILE

    @pl.when(step == 0)
    def _():
        load_keys(kv_refs, kv_all, sem, kv_all.shape[0] // blocks)

    acc[...] = jnp.zeros_like(acc)
    norm[...] = jnp.zeros_like(norm)

    @pl.loop(0, key_tiles)
    def _(t):
        @pl.when(flags_ref[step * key_tiles + t] > 0)
        def _():
            rows = pl.ds(pl.multiple_of(t * KEY_TILE, KEY_TILE), KEY_TILE)
            bias = bias_ref[:, rows]
            bias = jnp.concatenate([bias] * share, axis=0)
            for g in range(k_heads):
                keys = kv_all[rows, g * HEAD : (g + 1) * HEAD]
                values = kv_all[rows, (k_heads + g) * HEAD : (k_heads + g + 1) * HEAD]
                scores = matmul(stacked(q_ref, g, share), keys, ((1,), (1,)))
                weights = jnp.exp2(scores * (SCALE * LOG2E) + bias)
                norm[g] += jnp.sum(weights, axis=1, keepdims=True)
                acc[g] += matmul(weights.astype(BF16), values)

    lane = lax.broadcasted_iota(jnp.int32, (tile, LANES), 1)
    lse = jnp.zeros((tile, LANES), F32)
    for g in range(k_heads):
        total = norm[g]
        attended = acc[g] / total
        log_total = jnp.log2(total)
        for j in range(share):
            h = g * share + j
            here = slice(h * HEAD, (h + 1) * HEAD)
            part = attended[j * tile : (j + 1) * tile]
            att_out[:, here] = part
            gated_out[:, here] = (part * sg_ref[:, h : h + 1]).astype(BF16)
            lse = jnp.where(lane == h, log_total[j * tile : (j + 1) * tile], lse)
    lse_out[...] = lse


def attend(flags, tile, queries, bias, sg, kvs, q_heads, k_heads):
    rows = queries.shape[0]
    blocks = len(kvs)
    keys = sum(kv.shape[0] for kv in kvs)
    share = q_heads // k_heads

    def at(width):
        return pl.BlockSpec((tile, width), lambda i, flags: (i, 0))

    return pl.pallas_call(
        functools.partial(attend_kernel, q_heads, k_heads, blocks),
        grid_spec=pltpu.PrefetchScalarGridSpec(
            num_scalar_prefetch=1,
            grid=(rows // tile,),
            in_specs=[at(q_heads * HEAD), at(keys), at(LANES)]
            + [pl.BlockSpec(memory_space=pl.ANY)] * blocks,
            out_specs=[at(q_heads * HEAD), at(q_heads * HEAD), at(LANES)],
            scratch_shapes=[
                pltpu.VMEM((keys, 2 * k_heads * HEAD), BF16),
                pltpu.VMEM((k_heads, share * tile, HEAD), F32),
                pltpu.VMEM((k_heads, share * tile, 1), F32),
                pltpu.SemaphoreType.DMA((blocks,)),
            ],
        ),
        out_shape=[
            jax.ShapeDtypeStruct((rows, q_heads * HEAD), F32),
            jax.ShapeDtypeStruct((rows, q_heads * HEAD), BF16),
            jax.ShapeDtypeStruct((rows, LANES), F32),
        ],
        compiler_params=params(),
        cost_estimate=pl.CostEstimate(
            flops=2 * rows * keys * HEAD * q_heads * 2,
            bytes_accessed=rows * keys * 4,
            transcendentals=rows * keys * q_heads,
        ),
        name="attend",
    )(flags, queries, bias, sg, *kvs)


def attend_back_kernel(q_heads, k_heads, blocks, flags_ref, *refs):
    q_ref, bias_ref, sg_ref, lse_ref, att_ref, dgat_ref = refs[:6]
    kv_refs = refs[6 : 6 + blocks]
    dq_out, dlog_out, keep_out, send_out = refs[6 + blocks : 10 + blocks]
    kv_all, dkv, dq, dout, delta, lses, sem = refs[10 + blocks :]
    share = q_heads // k_heads
    tile = q_ref.shape[0]
    step = pl.program_id(0)
    key_tiles = kv_all.shape[0] // KEY_TILE

    @pl.when(step == 0)
    def _():
        load_keys(kv_refs, kv_all, sem, kv_all.shape[0] // blocks)
        dkv[...] = jnp.zeros_like(dkv)

    dq[...] = jnp.zeros_like(dq)
    lane = lax.broadcasted_iota(jnp.int32, (tile, LANES), 1)
    dlog = jnp.zeros((tile, LANES), F32)
    for h in range(q_heads):
        g, j = h // share, h % share
        here = slice(h * HEAD, (h + 1) * HEAD)
        there = slice(j * tile, (j + 1) * tile)
        sg = sg_ref[:, h : h + 1]
        dgat = dgat_ref[:, here]
        att = att_ref[:, here]
        rounded = (dgat * sg).astype(BF16)
        dout[g, there] = rounded
        delta[g, there] = jnp.sum(rounded.astype(F32) * att, axis=1, keepdims=True)
        lses[g, there] = lse_ref[:, h : h + 1]
        dlog_h = jnp.sum(dgat * att, axis=1, keepdims=True) * sg * (1.0 - sg)
        dlog = jnp.where(lane == h, dlog_h, dlog)
    dlog_out[...] = dlog.astype(BF16)

    @pl.loop(0, key_tiles)
    def _(t):
        @pl.when(flags_ref[step * key_tiles + t] > 0)
        def _():
            rows = pl.ds(pl.multiple_of(t * KEY_TILE, KEY_TILE), KEY_TILE)
            bias = bias_ref[:, rows]
            bias = jnp.concatenate([bias] * share, axis=0)
            for g in range(k_heads):
                k_here = slice(g * HEAD, (g + 1) * HEAD)
                v_here = slice((k_heads + g) * HEAD, (k_heads + g + 1) * HEAD)
                keys = kv_all[rows, k_here]
                values = kv_all[rows, v_here]
                queries = stacked(q_ref, g, share)
                scores = matmul(queries, keys, ((1,), (1,)))
                probs = jnp.exp2(scores * (SCALE * LOG2E) + bias - lses[g])
                dprobs = matmul(dout[g], values, ((1,), (1,)))
                dscores = (probs * (dprobs - delta[g])).astype(BF16)
                dkv[rows, v_here] += matmul(probs.astype(BF16), dout[g], ((0,), (0,)))
                dkv[rows, k_here] += matmul(dscores, queries, ((0,), (0,)))
                dq[g] += matmul(dscores, keys)

    for h in range(q_heads):
        g, j = h // share, h % share
        dq_out[:, h * HEAD : (h + 1) * HEAD] = dq[g, j * tile : (j + 1) * tile] * SCALE

    @pl.when(step == pl.num_programs(0) - 1)
    def _():
        half = kv_all.shape[0] // 2
        k_all = slice(0, k_heads * HEAD)
        v_all = slice(k_heads * HEAD, 2 * k_heads * HEAD)
        for out, first in ((keep_out, 0), (send_out, half)):
            out[:, k_all] = (dkv[first : first + half, k_all] * SCALE).astype(BF16)
            out[:, v_all] = dkv[first : first + half, v_all].astype(BF16)


def attend_back(flags, tile, queries, bias, sg, lse, att, dgat, kvs, q_heads, k_heads):
    rows = queries.shape[0]
    blocks = len(kvs)
    keys = sum(kv.shape[0] for kv in kvs)
    share = q_heads // k_heads
    kv_width = 2 * k_heads * HEAD

    def at(width):
        return pl.BlockSpec((tile, width), lambda i, flags: (i, 0))

    whole = pl.BlockSpec((keys // 2, kv_width), lambda i, flags: (0, 0))
    return pl.pallas_call(
        functools.partial(attend_back_kernel, q_heads, k_heads, blocks),
        grid_spec=pltpu.PrefetchScalarGridSpec(
            num_scalar_prefetch=1,
            grid=(rows // tile,),
            in_specs=[
                at(q_heads * HEAD),
                at(keys),
                at(LANES),
                at(LANES),
                at(q_heads * HEAD),
                at(q_heads * HEAD),
            ]
            + [pl.BlockSpec(memory_space=pl.ANY)] * blocks,
            out_specs=[at(q_heads * HEAD), at(LANES), whole, whole],
            scratch_shapes=[
                pltpu.VMEM((keys, kv_width), BF16),
                pltpu.VMEM((keys, kv_width), F32),
                pltpu.VMEM((k_heads, share * tile, HEAD), F32),
                pltpu.VMEM((k_heads, share * tile, HEAD), BF16),
                pltpu.VMEM((k_heads, share * tile, 1), F32),
                pltpu.VMEM((k_heads, share * tile, 1), F32),
                pltpu.SemaphoreType.DMA((blocks,)),
            ],
        ),
        out_shape=[
            jax.ShapeDtypeStruct((rows, q_heads * HEAD), F32),
            jax.ShapeDtypeStruct((rows, LANES), BF16),
            jax.ShapeDtypeStruct((keys // 2, kv_width), BF16),
            jax.ShapeDtypeStruct((keys // 2, kv_width), BF16),
        ],
        compiler_params=params(),
        cost_estimate=pl.CostEstimate(
            flops=2 * rows * keys * HEAD * q_heads * 5,
            bytes_accessed=rows * keys * 4,
            transcendentals=rows * keys * q_heads,
        ),
        name="attend_back",
    )(flags, queries, bias, sg, lse, att, dgat, *kvs)


def per_device(
    sizes,
    tokens,
    seg_ids,
    positions,
    cotangent,
    norm_in,
    norm_mid,
    query_gain,
    key_gain,
    query_weight,
    key_matrix,
    value_matrix,
    head_weight,
    out_weight,
    gate_weight,
    up_weight,
    down_weight,
):
    n_shard, n_ctx, n_tp = sizes
    ring = Ring(n_shard, n_ctx)
    row_count, width = tokens.shape
    block = query_weight.shape[0]
    q_width = query_weight.shape[1]
    k_width = key_matrix.shape[1]
    q_heads, k_heads = q_width // HEAD, k_width // HEAD
    units = gate_weight.shape[1]
    chunk = units // CHUNKS
    rows = row_count // n_tp
    tile = row_tile(rows)

    here_ctx = lax.axis_index("ctx")
    here_tp = lax.axis_index("tp")
    here = lax.axis_index("shard") * n_ctx + here_ctx
    order = lax.dynamic_index_in_dim(jnp.asarray(ring.order), here, keepdims=False)
    inverse = lax.dynamic_index_in_dim(
        jnp.asarray(np.argsort(ring.order, axis=1).astype(np.int32)), here, keepdims=False
    )
    per = rows // tile
    tile_ids = np.arange(row_count // tile)
    tiles = ((here_tp + tile_ids // per) % n_tp) * per + tile_ids % per
    tiles = tiles.astype(jnp.int32)

    columns = [
        head_weight,
        norm_in[:, None],
        norm_mid[:, None],
        jnp.pad(query_gain, (0, block - query_gain.shape[0]))[:, None],
        jnp.pad(key_gain, (0, block - key_gain.shape[0]))[:, None],
    ]
    extra = sum(column.shape[1] for column in columns)
    columns.append(jnp.zeros((block, LANES - extra), BF16))
    send_a = jnp.concatenate([query_weight] + columns, axis=1)
    send_b = jnp.concatenate([key_matrix, value_matrix], axis=1)
    pieces_a = ring.gather(send_a)
    pieces_b = ring.gather(send_b)
    pieces_o = ring.gather(after(out_weight.T, pieces_a[4]))
    pieces_gu, pieces_d = [], []
    gate_after = pieces_a[5]
    for j in range(CHUNKS):
        cut = slice(j * chunk, (j + 1) * chunk)
        both = jnp.concatenate([gate_weight[:, cut], up_weight[:, cut]], axis=1)
        down = down_weight[cut].T
        both, down, _ = lax.optimization_barrier((both, down, gate_after))
        pieces_gu.append(ring.gather(both))
        pieces_d.append(ring.gather(down))
        gate_after = pieces_gu[-1][4]

    tok, cot, scale_in = enter(order, tiles, tile, tokens, cotangent)
    offset = here_ctx * row_count

    def own_rows(values):
        parts = [
            lax.dynamic_slice_in_dim(values, offset + ((here_tp + j) % n_tp) * rows, rows)
            for j in range(n_tp)
        ]
        return jnp.concatenate(parts)

    own_seg, own_pos = own_rows(seg_ids), own_rows(positions)
    block_order = sorted(range(n_ctx), key=lambda m: (m & 1, m))

    def key_rows(values):
        return jnp.concatenate(
            [
                lax.dynamic_slice_in_dim(values, (here_ctx ^ m) * row_count, row_count)
                for m in block_order
            ]
        )

    key_seg, key_pos = key_rows(seg_ids), key_rows(positions)
    allowed = ((key_seg[None, :] == 0) | (key_seg[None, :] == own_seg[:, None])) & (
        key_pos[None, :] <= own_pos[:, None]
    )
    bias = jnp.where(allowed, 0.0, MASKED).astype(F32)
    key_tiles = key_seg.shape[0] // KEY_TILE
    flags = jnp.max(
        allowed.astype(jnp.int32).reshape(row_count // tile, tile, key_tiles, KEY_TILE), axis=(1, 3)
    ).reshape(-1)
    half = HEAD // 2
    frequency = THETA ** (-(jnp.arange(half, dtype=F32) * 2.0) / HEAD)
    angles = own_pos.astype(F32)[:, None] * frequency[None, :]
    cos, sin = jnp.cos(angles), jnp.sin(angles)
    cos = jnp.concatenate([cos, cos], axis=1)
    sin = jnp.concatenate([-sin, sin], axis=1)

    weight_a = ring.assemble(pieces_a)
    weight_b = ring.assemble(pieces_b)
    tail = weight_a[:, q_width:]
    n_head = head_weight.shape[1]
    gain_in = tail[:, n_head].astype(F32)[None, :]
    gain_mid = tail[:, n_head + 1].astype(F32)[None, :]

    def whole_gain(column):
        pieces = tail[:, column].reshape(-1, block)[:, : query_gain.shape[0]]
        return jnp.take(pieces, inverse, axis=0).reshape(1, HEAD).astype(F32)

    q_gain, k_gain = whole_gain(n_head + 2), whole_gain(n_head + 3)
    scale_in = scale_in[:, :1]
    normed = (tok.astype(F32) * scale_in * gain_in).astype(BF16)
    raw_a = matmul(normed, weight_a)
    raw_b = matmul(normed, weight_b)
    queries, kv, sg = make_heads(
        tiles, tile, raw_a, raw_b, cos, sin, q_gain, k_gain, q_heads, k_heads
    )
    kvs = {0: kv}
    bit = n_ctx // 2
    while bit:
        for m in list(kvs):
            kvs[m | bit] = lax.ppermute(kvs[m], "ctx", [(i, i ^ bit) for i in range(n_ctx)])
        bit //= 2
    kvs = [kvs[m] for m in block_order]
    att, gated, lse = attend(flags, tile, queries, bias, sg, kvs, q_heads, k_heads)
    weight_o = ring.assemble(pieces_o)
    branch = tp_scatter(matmul(gated, weight_o, ((1,), (1,))), n_tp)
    middle = tok[:rows].astype(F32) + branch
    scale_mid = lax.rsqrt(jnp.mean(middle * middle, axis=-1, keepdims=True) + EPS)
    unit_mid = middle * scale_mid
    normed_mid = jnp.concatenate(tp_gather((unit_mid * gain_mid).astype(BF16), n_tp))

    own_cols = slice(0, width // 2)
    other_cols = slice(width // 2, width)

    def weight_grad(left, right):
        sent = matmul(left[:, other_cols], right, ((0,), (0,))).astype(BF16)
        kept = matmul(left[:, own_cols], right, ((0,), (0,)))
        return (kept + ring.swap(sent).astype(F32)).astype(BF16)

    mixed = None
    grad_mid = None
    sums_gu, sums_d = [], []
    for j in range(CHUNKS):
        weight_gu = ring.assemble(pieces_gu[j])
        weight_d = ring.assemble(pieces_d[j])
        both = matmul(normed_mid, weight_gu)
        gate, up = both[:, :chunk], both[:, chunk:]
        dhidden = matmul(cot, weight_d)
        sig = jax.nn.sigmoid(gate)
        hidden = (gate * sig * up).astype(BF16)
        dgate = (dhidden * up * sig * (1.0 + gate * (1.0 - sig))).astype(BF16)
        dup = (dhidden * gate * sig).astype(BF16)
        dboth = jnp.concatenate([dgate, dup], axis=1)
        sums_d.append(ring.reduce(weight_grad(cot, hidden)))
        sums_gu.append(ring.reduce(weight_grad(normed_mid, dboth)))
        part = matmul(hidden, weight_d, ((1,), (1,)))
        mixed = part if mixed is None else mixed + part
        part = matmul(dboth, weight_gu, ((1,), (1,)))
        grad_mid = part if grad_mid is None else grad_mid + part

    def norm_back(grad_unit, unit, scale):
        return scale * (grad_unit - unit * jnp.mean(grad_unit * unit, axis=-1, keepdims=True))

    dmid = cot[:rows].astype(F32) + norm_back(
        tp_scatter(grad_mid, n_tp) * gain_mid, unit_mid, scale_mid
    )
    dmid_low = jnp.concatenate(tp_gather(dmid.astype(BF16), n_tp))
    output = (middle + tp_scatter(mixed, n_tp)).astype(BF16)
    output = leave(order, tiles, tile, jnp.concatenate(tp_gather(output, n_tp)), BF16, "leave_output")

    dgat = matmul(dmid_low, weight_o)
    sum_o = ring.reduce(weight_grad(dmid_low, gated))
    dq, dlog, keep, sent = attend_back(
        flags, tile, queries, bias, sg, lse, att, dgat, kvs, q_heads, k_heads
    )
    other = ring.swap(sent)
    blocks = n_ctx // 2
    mine = keep[:row_count]
    theirs = other[:row_count]
    arrived = []
    for k in range(1, blocks):
        piece = slice(k * row_count, (k + 1) * row_count)
        away = (keep[piece].astype(F32) + other[piece].astype(F32)).astype(BF16)
        m = block_order[k]
        arrived.append(lax.ppermute(away, "ctx", [(i, i ^ m) for i in range(n_ctx)]))
    while len(arrived) > 1:
        arrived = [(arrived[0].astype(F32) + arrived[1].astype(F32)).astype(BF16)] + arrived[2:]
    d_a, d_b, gain_sums = heads_back(
        tiles,
        tile,
        dq,
        [mine, theirs, arrived[0]],
        dlog,
        raw_a,
        raw_b,
        cos,
        sin,
        q_gain,
        k_gain,
        q_heads,
        k_heads,
    )
    gain_size = query_gain.shape[0]

    def gain_column(row):
        pieces = jnp.take(gain_sums[row].reshape(-1, gain_size), order, axis=0)
        return jnp.pad(pieces, ((0, 0), (0, block - gain_size))).reshape(-1, 1)

    lane = lax.broadcasted_iota(jnp.int32, (1, d_a.shape[1]), 1)
    extra_a = jnp.where(lane == q_width + n_head, gain_column(0), 0.0) + jnp.where(
        lane == q_width + n_head + 1, gain_column(1), 0.0
    )
    sent_a = (matmul(normed[:, other_cols], d_a, ((0,), (0,))) + extra_a[width // 2 :]).astype(BF16)
    kept_a = matmul(normed[:, own_cols], d_a, ((0,), (0,))) + extra_a[: width // 2]
    sum_a = ring.reduce((kept_a + ring.swap(sent_a).astype(F32)).astype(BF16))
    sum_b = ring.reduce(weight_grad(normed, d_b))
    grad_normed = matmul(d_a, weight_a, ((1,), (1,))) + matmul(d_b, weight_b, ((1,), (1,)))
    unit_in = tok[:rows].astype(F32) * scale_in[:rows]
    dtok = dmid + norm_back(tp_scatter(grad_normed, n_tp) * gain_in, unit_in, scale_in[:rows])
    dtok = jnp.concatenate(tp_gather(dtok.astype(BF16), n_tp))
    input_grad = leave(order, tiles, tile, dtok, F32, "leave_grad")

    sum_gate = jnp.concatenate([both[:, :chunk] for both in sums_gu], axis=1)
    sum_up = jnp.concatenate([both[:, chunk:] for both in sums_gu], axis=1)
    sum_down = jnp.concatenate(sums_d, axis=1).T
    mid_share = jnp.sum(sum_gate * gate_weight.astype(F32), axis=1) + jnp.sum(
        sum_up * up_weight.astype(F32), axis=1
    )
    in_share = (
        jnp.sum(sum_a[:, :q_width] * query_weight.astype(F32), axis=1)
        + jnp.sum(sum_b[:, :k_width] * key_matrix.astype(F32), axis=1)
        + jnp.sum(sum_b[:, k_width:] * value_matrix.astype(F32), axis=1)
        + jnp.sum(sum_a[:, q_width : q_width + n_head] * head_weight.astype(F32), axis=1)
    )
    small = jnp.stack(
        [
            in_share / norm_in.astype(F32),
            mid_share / norm_mid.astype(F32),
            sum_a[:, q_width + n_head],
            sum_a[:, q_width + n_head + 1],
        ]
    )
    small = tp_total(small, n_tp)
    return (
        output,
        input_grad,
        small[0],
        small[1],
        small[2, :gain_size],
        small[3, :gain_size],
        sum_a[:, :q_width],
        sum_b[:, :k_width],
        sum_b[:, k_width:],
        sum_a[:, q_width : q_width + n_head],
        sum_o.T,
        sum_gate,
        sum_up,
        sum_down,
    )


def solution(mesh):
    sizes = (mesh.shape["shard"], mesh.shape["ctx"], mesh.shape["tp"])
    split = ("shard", "ctx")
    rows = P(split, None)
    vector = P(split)
    weight = P(split, "tp")
    turned = P("tp", split)
    return jax.shard_map(
        functools.partial(per_device, sizes),
        mesh=mesh,
        in_specs=(rows, P("shard"), P("shard"), rows)
        + (vector,) * 4
        + (weight,) * 4
        + (turned, weight, weight, turned),
        out_specs=(rows, rows) + (vector,) * 4 + (weight,) * 4 + (turned, weight, weight, turned),
        check_vma=False,
    )
```

```python
import functools

import jax
import jax.numpy as jnp
import numpy as np
from jax import lax
from jax.experimental import pallas as pl
from jax.experimental.pallas import tpu as pltpu
from jax.sharding import PartitionSpec as P

HEAD = 128
LANES = 128
EPS = 1e-06
THETA = 1000000.0
MASKED = -1e30
LOG2E = 1.4426950408889634
SCALE = HEAD ** (-0.5)
KEY_TILE = 256
CHUNKS = 3
COLUMN_TILE = 256
ROW_TILE = 128
FORWARD_HEADS = 4
BACKWARD_HEADS = 2
GAINS = 64

F32 = jnp.float32
BF16 = jnp.bfloat16


def matmul(a, b, dims=((1,), (0,))):
    return lax.dot_general(a, b, (dims, ((), ())), preferred_element_type=F32)


def ring_tables(n_shard, n_ctx):
    path = []
    for x in range(n_ctx // 2):
        column = range(n_shard) if x % 2 == 0 else reversed(range(n_shard))
        path += [(z, x) for z in column]
    length = len(path)

    def device(place, core):
        z, x = path[place % length]
        return z * n_ctx + x * 2 + core

    hops = [(device(r, 0), device(r + 1, 0)) for r in range(length)]
    hops += [(device(r, 1), device(r - 1, 1)) for r in range(length)]
    order = np.zeros((n_shard * n_ctx, 2 * length), np.int32)
    for r in range(length):
        for core in (0, 1):
            back = -1 if core == 0 else 1
            order[device(r, core), 0::2] = [device(r + back * s, core) for s in range(length)]
            order[device(r, core), 1::2] = [device(r - back * s, 1 - core) for s in range(length)]
    return hops, order, length


def hold(value, *others):
    others = [other for other in others if other is not None]
    return lax.optimization_barrier((value, *others))[0] if others else value


class Ring:
    def __init__(self, n_shard, n_ctx):
        self.hops, self.order, self.length = ring_tables(n_shard, n_ctx)
        self.swaps = [(i, i ^ 1) for i in range(n_ctx)]

    def hop(self, value):
        return lax.ppermute(value, ("shard", "ctx"), self.hops)

    def swap(self, value):
        return lax.ppermute(value, "ctx", self.swaps)


class Gather:
    def __init__(self, ring, block):
        self.ring = ring
        self.last = block
        self.pieces = [block, ring.swap(block)]

    def step(self, *others):
        if len(self.pieces) < 2 * self.ring.length:
            self.last = self.ring.hop(hold(self.last, *others))
            self.pieces += [self.last, self.ring.swap(self.last)]
        return self.last


class Reduce:
    def __init__(self, ring, kept, sent):
        self.ring = ring
        self.rows = kept.shape[0] // ring.length
        self.kept = kept
        self.other = ring.swap(sent)
        self.place = 1
        self.total = self.own().astype(BF16)

    def own(self):
        first = (self.place % self.ring.length) * self.rows
        here = slice(first, first + self.rows)
        return self.kept[here].astype(F32) + self.other[here].astype(F32)

    def step(self, *others):
        if self.place < self.ring.length:
            self.place += 1
            total = self.ring.hop(hold(self.total, *others)).astype(F32) + self.own()
            self.total = total if self.place == self.ring.length else total.astype(BF16)
        return self.total

    def finish(self):
        while self.place < self.ring.length:
            self.step()
        return self.total


def tp_send(sent, rows, n_tp):
    return [
        lax.ppermute(
            sent[(j - 1) * rows : j * rows], "tp", [(i, (i + j) % n_tp) for i in range(n_tp)]
        )
        for j in range(1, n_tp)
    ]


def tp_gather(block, n_tp):
    blocks = [block]
    for j in range(1, n_tp):
        blocks.append(lax.ppermute(block, "tp", [(i, (i - j) % n_tp) for i in range(n_tp)]))
    return blocks


def tp_total(value, n_tp):
    total = value
    for j in range(1, n_tp):
        total = total + lax.ppermute(value, "tp", [(i, (i + j) % n_tp) for i in range(n_tp)])
    return total


def row_tile(rows):
    return next(tile for tile in (128, 96, 64, 48, 32, 16) if rows % tile == 0)


def params(mib=56):
    return pltpu.CompilerParams(vmem_limit_bytes=mib << 20)


def cost(flops, moved, transcendentals=0):
    return pl.CostEstimate(flops=flops, bytes_accessed=moved, transcendentals=transcendentals)


def fixed(shape):
    return pl.BlockSpec(shape, lambda *_: (0,) * len(shape), pipeline_mode=pl.Buffered(1))


def shaped(shape, dtype):
    return jax.ShapeDtypeStruct(shape, dtype)


def enter_kernel(order_ref, rows_ref, tok_ref, cot_ref, tok_out, cot_out, scale_out):
    value = tok_ref[...].astype(F32)
    scale = lax.rsqrt(jnp.mean(value * value, axis=-1, keepdims=True) + EPS)
    scale_out[...] = jnp.broadcast_to(scale, scale_out.shape)
    for j in range(tok_ref.shape[1] // LANES):
        source = pl.multiple_of(order_ref[j] * LANES, LANES)
        here = slice(j * LANES, (j + 1) * LANES)
        tok_out[:, here] = tok_ref[:, pl.ds(source, LANES)]
        cot_out[:, here] = cot_ref[:, pl.ds(source, LANES)]


def enter(order, tiles, tile, tokens, cotangent):
    rows, width = tokens.shape
    block = pl.BlockSpec((tile, width), lambda i, order, tiles: (tiles[i], 0))
    out = pl.BlockSpec((tile, width), lambda i, order, tiles: (i, 0))
    return pl.pallas_call(
        enter_kernel,
        grid_spec=pltpu.PrefetchScalarGridSpec(
            num_scalar_prefetch=2,
            grid=(rows // tile,),
            in_specs=[block, block],
            out_specs=[out, out, pl.BlockSpec((tile, LANES), lambda i, order, tiles: (i, 0))],
        ),
        out_shape=[
            shaped((rows, width), BF16),
            shaped((rows, width), BF16),
            shaped((rows, LANES), F32),
        ],
        compiler_params=params(),
        cost_estimate=cost(rows * width * 4, rows * width * 8),
        name="enter",
    )(order, tiles, tokens, cotangent)


def leave_kernel(parts, order_ref, tiles_ref, *refs):
    out_ref = refs[parts]
    per = pl.num_programs(0) // parts
    for k in range(parts):

        @pl.when(pl.program_id(0) // per == k)
        def _():
            for j in range(out_ref.shape[1] // LANES):
                target = pl.multiple_of(order_ref[j] * LANES, LANES)
                out_ref[:, pl.ds(target, LANES)] = refs[k][
                    :, j * LANES : (j + 1) * LANES
                ].astype(out_ref.dtype)


def leave(order, tiles, tile, parts, dtype, name):
    rows, width = parts[0].shape
    per = rows // tile
    total = rows * len(parts)

    def part(k):
        return pl.BlockSpec(
            (tile, width), lambda i, order, tiles: (jnp.clip(i - k * per, 0, per - 1), 0)
        )

    return pl.pallas_call(
        functools.partial(leave_kernel, len(parts)),
        grid_spec=pltpu.PrefetchScalarGridSpec(
            num_scalar_prefetch=2,
            grid=(total // tile,),
            in_specs=[part(k) for k in range(len(parts))],
            out_specs=pl.BlockSpec((tile, width), lambda i, order, tiles: (tiles[i], 0)),
        ),
        out_shape=shaped((total, width), dtype),
        compiler_params=params(),
        cost_estimate=cost(0, total * width * 6),
        name=name,
    )(order, tiles, *parts)


def gains_kernel(order_ref, *refs):
    pieces, (wide_out, head_out) = refs[:-2], refs[-2:]
    size = HEAD // len(pieces)
    total = jnp.zeros((8, HEAD), F32)
    for j, piece in enumerate(pieces):
        turned = jnp.transpose(piece[...].astype(F32))[GAINS : GAINS + 8]
        wide_out[:, j * LANES : (j + 1) * LANES] = turned
        total += pltpu.roll(turned, order_ref[j] * size, 1)
    head_out[...] = total


def gather_gains(order, pieces, q_width):
    count = len(pieces)
    block = pieces[0].shape[0]
    spec = pl.BlockSpec((block, LANES), lambda i, order: (0, q_width // LANES))
    return pl.pallas_call(
        gains_kernel,
        grid_spec=pltpu.PrefetchScalarGridSpec(
            num_scalar_prefetch=1,
            grid=(1,),
            in_specs=[spec] * count,
            out_specs=[
                pl.BlockSpec((8, block * count), lambda i, order: (0, 0)),
                pl.BlockSpec((8, HEAD), lambda i, order: (0, 0)),
            ],
        ),
        out_shape=[shaped((8, block * count), F32), shaped((8, HEAD), F32)],
        compiler_params=params(),
        cost_estimate=cost(0, block * count * LANES * 2),
        name="gather_gains",
    )(order, *pieces)


def turn(value, cos, sin):
    return value * cos + pltpu.roll(value, HEAD // 2, 1) * sin


def project_kernel(q_heads, k_heads, count, tiles_ref, *refs):
    tok_ref, scale_ref, wide_ref, head_ref, cos_ref, sin_ref = refs[:6]
    a_refs, b_refs = refs[6 : 6 + count], refs[6 + count : 6 + 2 * count]
    normed_out, a_out, b_out, q_out, kv_out, sg_out = refs[6 + 2 * count :]
    cos, sin = cos_ref[...], sin_ref[...]
    normed = (tok_ref[...].astype(F32) * scale_ref[:, :1] * wide_ref[0:1, :]).astype(BF16)
    normed_out[...] = normed

    def rotated(value, gain):
        scale = lax.rsqrt(jnp.mean(value * value, axis=-1, keepdims=True) + EPS)
        return turn(value * scale * gain, cos, sin).astype(BF16)

    def product(refs, here):
        return matmul(normed_out[...], jnp.concatenate([ref[:, here] for ref in refs], axis=0))

    q_width, k_width = q_heads * HEAD, k_heads * HEAD
    q_tile, k_tile = min(COLUMN_TILE, q_width), min(COLUMN_TILE, k_width)

    @pl.loop(0, q_width // q_tile, unroll=True)
    def _(i):
        here = pl.ds(pl.multiple_of(i * q_tile, q_tile), q_tile)
        value = product(a_refs, here)
        a_out[:, here] = value
        q_out[:, here] = jnp.concatenate(
            [
                rotated(value[:, h * HEAD : (h + 1) * HEAD], head_ref[2:3, :])
                for h in range(q_tile // HEAD)
            ],
            axis=1,
        )

    tail = slice(q_width, q_width + LANES)
    value = product(a_refs, tail)
    a_out[:, tail] = value
    sg_out[...] = jax.nn.sigmoid(value)

    @pl.loop(0, k_width // k_tile, unroll=True)
    def _(i):
        here = pl.ds(pl.multiple_of(i * k_tile, k_tile), k_tile)
        value = product(b_refs, here)
        b_out[:, here] = value
        kv_out[:, here] = jnp.concatenate(
            [
                rotated(value[:, h * HEAD : (h + 1) * HEAD], head_ref[3:4, :])
                for h in range(k_tile // HEAD)
            ],
            axis=1,
        )

    @pl.loop(0, k_width // k_tile, unroll=True)
    def _(i):
        here = pl.ds(pl.multiple_of(k_width + i * k_tile, k_tile), k_tile)
        value = product(b_refs, here)
        b_out[:, here] = value
        kv_out[:, here] = value.astype(BF16)


def project(tiles, tile, tok, scale, wide, head, cos, sin, pieces_a, pieces_b, q_heads, k_heads):
    rows, width = tok.shape
    count = len(pieces_a)
    a_width, b_width = pieces_a[0].shape[1], pieces_b[0].shape[1]

    def at(width):
        return pl.BlockSpec((tile, width), lambda i, tiles: (i, 0))

    return pl.pallas_call(
        functools.partial(project_kernel, q_heads, k_heads, count),
        grid_spec=pltpu.PrefetchScalarGridSpec(
            num_scalar_prefetch=1,
            grid=(rows // tile,),
            in_specs=[at(width), at(LANES), fixed(wide.shape), fixed(head.shape), at(HEAD), at(HEAD)]
            + [fixed(piece.shape) for piece in pieces_a + pieces_b],
            out_specs=[
                at(width),
                at(a_width),
                at(b_width),
                at(q_heads * HEAD),
                pl.BlockSpec((tile, 2 * k_heads * HEAD), lambda i, tiles: (tiles[i], 0)),
                at(LANES),
            ],
        ),
        out_shape=[
            shaped((rows, width), BF16),
            shaped((rows, a_width), F32),
            shaped((rows, b_width), F32),
            shaped((rows, q_heads * HEAD), BF16),
            shaped((rows, 2 * k_heads * HEAD), BF16),
            shaped((rows, LANES), F32),
        ],
        compiler_params=params(),
        cost_estimate=cost(
            2 * rows * width * (a_width + b_width), width * (a_width + b_width) * 2 + rows * width * 16
        ),
        name="project",
    )(tiles, tok, scale, wide, head, cos, sin, *pieces_a, *pieces_b)


def spread_kernel(terms, count, rows, has_start, split, *refs):
    used = 0
    groups = []
    for width, _ in terms:
        groups.append((refs[used], refs[used + 1 : used + 1 + count]))
        used += 1 + count
    start_ref = None
    if has_start:
        start_ref = refs[used]
        used += 1
    outs = 2 if split else 1
    out_refs, scratch = refs[used : used + outs], refs[used + outs :]
    bufs, sem = scratch[:-1], scratch[-1]
    step = pl.program_id(0)
    block = groups[0][1][0].shape[0]

    def copies(s):
        slot = s % 2
        found = []
        for t, (width, offset) in enumerate(terms):
            for k in range(2):
                found.append(
                    pltpu.make_async_copy(
                        groups[t][1][2 * s + k].at[:, pl.ds(offset, width)],
                        bufs[t].at[slot, pl.ds(k * block, block)],
                        sem.at[slot, 2 * t + k],
                    )
                )
        return found

    for s in range(count // 2):

        @pl.when(step == s)
        def _():
            if s == 0:
                for copy in copies(0):
                    copy.start()
            if s + 1 < count // 2:
                for copy in copies(s + 1):
                    copy.start()
            for copy in copies(s):
                copy.wait()

    slot = lax.rem(step, 2)
    total = None
    for t in range(len(terms)):
        part = matmul(groups[t][0][...], bufs[t][slot], ((1,), (1,)))
        total = part if total is None else total + part
    if has_start:
        total = total + start_ref[...]
    if split:
        out_refs[0][...] = total[:rows]
        out_refs[1][...] = total[rows:].astype(BF16)
    else:
        out_refs[0][...] = total


def spread(terms, rows, name, start=None, split=True):
    count = len(terms[0][1])
    block = terms[0][1][0].shape[0]
    total = terms[0][0].shape[0]
    width = block * count
    sizes = [(x.shape[1], offset) for x, _, offset in terms]
    operands, specs = [], []
    for x, pieces, _ in terms:
        operands += [x, *pieces]
        specs += [fixed(x.shape)] + [pl.BlockSpec(memory_space=pl.ANY)] * count
    column = pl.BlockSpec((total, 2 * block), lambda s: (0, s))
    if start is not None:
        operands.append(start)
        specs.append(column)
    if split:
        out_specs = [
            pl.BlockSpec((rows, 2 * block), lambda s: (0, s)),
            pl.BlockSpec((total - rows, 2 * block), lambda s: (0, s)),
        ]
        out_shape = [shaped((rows, width), F32), shaped((total - rows, width), BF16)]
    else:
        out_specs, out_shape = [column], [shaped((total, width), F32)]
    depth = sum(size for size, _ in sizes)
    return pl.pallas_call(
        functools.partial(spread_kernel, sizes, count, rows, start is not None, split),
        grid=(count // 2,),
        in_specs=specs,
        out_specs=out_specs,
        out_shape=out_shape,
        scratch_shapes=[pltpu.VMEM((2, 2 * block, size), BF16) for size, _ in sizes]
        + [pltpu.SemaphoreType.DMA((2, 2 * len(sizes)))],
        compiler_params=params(),
        cost_estimate=cost(2 * total * depth * width, depth * width * 2 + total * width * 6),
        name=name,
    )(*operands)


def units_kernel(parts, count, *refs):
    n_refs, c_ref = refs[:parts], refs[parts]
    weights = refs[parts + 1 : parts + 1 + 3 * count]
    hid_out, dgate_out, dup_out = refs[parts + 1 + 3 * count :]

    def weight(k):
        return jnp.concatenate([ref[...] for ref in weights[k * count : (k + 1) * count]], axis=0)

    rows = n_refs[0].shape[0]
    w_gate, w_up, w_down = weight(0), weight(1), weight(2)
    for k in range(parts):
        here = slice(k * rows, (k + 1) * rows)
        gate = matmul(n_refs[k][...], w_gate)
        up = matmul(n_refs[k][...], w_up)
        dhid = matmul(c_ref[here], w_down)
        sig = jax.nn.sigmoid(gate)
        silu = gate * sig
        hid_out[here] = (silu * up).astype(BF16)
        dgate_out[here] = (dhid * up * sig * (1.0 + gate * (1.0 - sig))).astype(BF16)
        dup_out[here] = (dhid * silu).astype(BF16)


def ff_units(normed, cot, pieces, offset, chunk):
    rows, width = cot.shape
    count = len(pieces)
    block = pieces[0].shape[0]
    specs, operands = [], []
    for k in range(3):
        first = (offset + k * chunk) // COLUMN_TILE
        specs += [pl.BlockSpec((block, COLUMN_TILE), lambda i, first=first: (0, first + i))] * count
        operands += pieces
    out = pl.BlockSpec((rows, COLUMN_TILE), lambda i: (0, i))
    return pl.pallas_call(
        functools.partial(units_kernel, len(normed), count),
        grid=(chunk // COLUMN_TILE,),
        in_specs=[fixed(part.shape) for part in normed] + [fixed(cot.shape)] + specs,
        out_specs=[out] * 3,
        out_shape=[shaped((rows, chunk), BF16)] * 3,
        compiler_params=params(),
        cost_estimate=cost(
            6 * rows * width * chunk, 3 * width * chunk * 2 + rows * width * 4, rows * chunk
        ),
        name="ff_units",
    )(*normed, cot, *operands)


def attended_back_kernel(parts, count, *refs):
    weights = refs[parts : parts + count]
    att_ref, sg_ref = refs[parts + count : parts + count + 2]
    dout_out, delta_out, dlog_out, dgat = refs[parts + count + 2 :]
    step = pl.program_id(0)

    @pl.when(step == 0)
    def _():
        delta_out[...] = jnp.zeros_like(delta_out)
        dlog_out[...] = jnp.zeros_like(dlog_out)

    weight = jnp.concatenate([ref[...] for ref in weights], axis=0)
    rows = refs[0].shape[0]
    for k in range(parts):
        dgat[k * rows : (k + 1) * rows] = matmul(refs[k][...], weight)
    lane = lax.broadcasted_iota(jnp.int32, (ROW_TILE, LANES), 1)
    place = lax.broadcasted_iota(jnp.int32, (delta_out.shape[0], ROW_TILE), 0)
    for r in range(dgat.shape[0] // ROW_TILE):
        there = slice(r * ROW_TILE, (r + 1) * ROW_TILE)
        dlog = dlog_out[there].astype(F32)
        delta = delta_out[:, there]
        for j in range(COLUMN_TILE // HEAD):
            head = step * (COLUMN_TILE // HEAD) + j
            here = slice(j * HEAD, (j + 1) * HEAD)
            sg = jnp.sum(jnp.where(lane == head, sg_ref[there], 0.0), axis=1, keepdims=True)
            grad = dgat[there, here]
            att = att_ref[there, here]
            rounded = (grad * sg).astype(BF16)
            dout_out[there, here] = rounded
            turned = jnp.transpose(rounded.astype(F32) * att)
            delta = jnp.where(place == head, jnp.sum(turned, axis=0, keepdims=True), delta)
            dlog_h = jnp.sum(grad * att, axis=1, keepdims=True) * sg * (1.0 - sg)
            dlog = jnp.where(lane == head, dlog_h, dlog)
        dlog_out[there] = dlog.astype(BF16)
        delta_out[:, there] = delta


def attended_back(lefts, pieces, att, sg):
    count = len(pieces)
    block = pieces[0].shape[0]
    rows = lefts[0].shape[0] * len(lefts)
    width = att.shape[1]
    column = pl.BlockSpec((rows, COLUMN_TILE), lambda i: (0, i))
    delta_rows = max(8, width // HEAD)
    return pl.pallas_call(
        functools.partial(attended_back_kernel, len(lefts), count),
        grid=(width // COLUMN_TILE,),
        in_specs=[fixed(left.shape) for left in lefts]
        + [pl.BlockSpec((block, COLUMN_TILE), lambda i: (0, i))] * count
        + [column, fixed(sg.shape)],
        out_specs=[
            column,
            pl.BlockSpec((delta_rows, rows), lambda i: (0, 0)),
            pl.BlockSpec((rows, LANES), lambda i: (0, 0)),
        ],
        out_shape=[
            shaped((rows, width), BF16),
            shaped((delta_rows, rows), F32),
            shaped((rows, LANES), BF16),
        ],
        scratch_shapes=[pltpu.VMEM((rows, COLUMN_TILE), F32)],
        compiler_params=params(),
        cost_estimate=cost(2 * rows * block * count * width, block * count * width * 2 + rows * width * 10),
        name="attended_back",
    )(*lefts, *pieces, att, sg)


def flip_kernel(*refs):
    rows = refs[0].shape[0]
    for k, ref in enumerate(refs[:-1]):
        refs[-1][:, k * rows : (k + 1) * rows] = jnp.transpose(ref[...])


def flip(parts, name):
    rows, width = parts[0].shape
    return pl.pallas_call(
        flip_kernel,
        grid=(width // COLUMN_TILE,),
        in_specs=[pl.BlockSpec((rows, COLUMN_TILE), lambda i: (0, i))] * len(parts),
        out_specs=pl.BlockSpec((COLUMN_TILE, rows * len(parts)), lambda i: (i, 0)),
        out_shape=shaped((width, rows * len(parts)), BF16),
        compiler_params=params(),
        cost_estimate=cost(0, rows * width * len(parts) * 4),
        name=name,
    )(*parts)


def outer_kernel(which, steps, gained, *refs):
    used = 0
    order_ref = gain_ref = None
    if gained is not None:
        order_ref, gain_ref = refs[0], refs[1]
        used = 2
    n_left = max(which) + 1
    lefts = refs[used : used + n_left]
    rights = refs[used + n_left : used + n_left + len(which)]
    kept_out, sent_out = refs[used + n_left + len(which) :]
    step = pl.program_id(0)
    count = lefts[0].shape[0] // LANES
    for k, left in enumerate(which):

        @pl.when(step // steps == k)
        def _():
            for j in range(count // 2):
                there = slice(2 * j * LANES, (2 * j + 2) * LANES)
                total = matmul(lefts[left][there], rights[k][...]).astype(BF16)
                kept_out[j * LANES : (j + 1) * LANES] = total[:LANES]
                sent_out[j * LANES : (j + 1) * LANES] = total[LANES:]

    if gained is not None:
        size = HEAD // count
        lane = lax.broadcasted_iota(jnp.int32, (16, LANES), 1)
        row = lax.broadcasted_iota(jnp.int32, (16, LANES), 0)
        tile = kept_out.shape[1]

        @pl.when(step == gained // tile)
        def _():
            there = slice(gained % tile, gained % tile + LANES)
            for j in range(count):
                more = jnp.zeros((16, LANES), F32)
                for k in range(2):
                    sums = jnp.broadcast_to(gain_ref[k : k + 1, :], (16, LANES))
                    picked = (lane == order_ref[j] * size + row) & (row < size)
                    column = jnp.sum(jnp.where(picked, sums, 0.0), axis=1, keepdims=True)
                    more += jnp.where(lane == GAINS + 2 + k, column, 0.0)
                out = kept_out if j % 2 == 0 else sent_out
                here = slice((j // 2) * LANES, (j // 2) * LANES + 16)
                out[here, there] = (out[here, there].astype(F32) + more).astype(BF16)


def outer(lefts, rights, which, name, gains=None, gained=None):
    width, rows = lefts[0].shape
    size = rights[0].shape[1]
    tile = next(tile for tile in (384, 256, 128) if size % tile == 0)
    if len(rights) > 1:
        tile = COLUMN_TILE
    steps = size // tile
    specs, operands = [], []
    if gained is not None:
        operands += list(gains)
        specs += [pl.BlockSpec(memory_space=pltpu.SMEM), fixed(gains[1].shape)]
    operands += list(lefts) + list(rights)
    specs += [fixed(left.shape) for left in lefts]
    for k in range(len(rights)):
        specs.append(
            pl.BlockSpec((rows, tile), lambda i, k=k: (0, jnp.clip(i - k * steps, 0, steps - 1)))
        )
    total = size * len(rights)
    out = pl.BlockSpec((width // 2, tile), lambda i: (0, i))
    return pl.pallas_call(
        functools.partial(outer_kernel, which, steps, gained),
        grid=(steps * len(rights),),
        in_specs=specs,
        out_specs=[out, out],
        out_shape=[shaped((width // 2, total), BF16)] * 2,
        compiler_params=params(),
        cost_estimate=cost(2 * rows * width * total, width * total * 2 + rows * (width + total) * 2),
        name=name,
    )(*operands)


def arrived_sum(own_ref, refs):
    total = own_ref[...]
    for ref in refs:
        total = total + ref[...].astype(F32)
    return total


def mean_of(value):
    return jnp.mean(value, axis=-1, keepdims=True)


def middle_kernel(own_ref, tok_ref, wide_ref, *refs):
    middle_out, normed_out = refs[-2:]
    middle = tok_ref[...].astype(F32) + arrived_sum(own_ref, refs[:-2])
    middle_out[...] = middle
    scale = lax.rsqrt(mean_of(middle * middle) + EPS)
    normed_out[...] = (middle * scale * wide_ref[1:2, :]).astype(BF16)


def middle_back_kernel(own_ref, cot_ref, middle_ref, wide_ref, *refs):
    dmid_out, low_out = refs[-2:]
    middle = middle_ref[...]
    scale = lax.rsqrt(mean_of(middle * middle) + EPS)
    unit = middle * scale
    grad = arrived_sum(own_ref, refs[:-2]) * wide_ref[1:2, :]
    dmid = cot_ref[...].astype(F32) + scale * (grad - unit * mean_of(grad * unit))
    dmid_out[...] = dmid
    low_out[...] = dmid.astype(BF16)


def output_kernel(own_ref, middle_ref, *refs):
    refs[-1][...] = (middle_ref[...] + arrived_sum(own_ref, refs[:-1])).astype(BF16)


def input_back_kernel(own_ref, tok_ref, scale_ref, dmid_ref, wide_ref, *refs):
    scale = scale_ref[:, :1]
    unit = tok_ref[...].astype(F32) * scale
    grad = arrived_sum(own_ref, refs[:-1]) * wide_ref[0:1, :]
    refs[-1][...] = (dmid_ref[...] + scale * (grad - unit * mean_of(grad * unit))).astype(BF16)


def by_rows(kernel, rows, tile, operands, wide, arrived, dtypes, name):
    width = operands[0].shape[1]

    def at(operand):
        return pl.BlockSpec((tile, operand.shape[1]), lambda i: (i, 0))

    specs = [at(operand) for operand in operands]
    if wide is not None:
        specs.append(fixed(wide.shape))
        operands = operands + [wide]
    specs += [at(operand) for operand in arrived]
    out = pl.BlockSpec((tile, width), lambda i: (i, 0))
    return pl.pallas_call(
        kernel,
        grid=(rows // tile,),
        in_specs=specs,
        out_specs=[out] * len(dtypes),
        out_shape=[shaped((rows, width), dtype) for dtype in dtypes],
        compiler_params=params(),
        cost_estimate=cost(rows * width * 12, rows * width * 14),
        name=name,
    )(*operands, *arrived)


def heads_back_kernel(q_heads, k_heads, groups, tiles_ref, *refs):
    dq_refs = refs[:groups]
    dkv_refs = refs[groups : 4 * groups]
    dlog_refs = refs[4 * groups : 5 * groups]
    a_ref, b_ref, cos_ref, sin_ref, head_ref = refs[5 * groups : 5 * groups + 5]
    a_out, b_out, gain_out = refs[5 * groups + 5 :]

    @pl.when(pl.program_id(0) == 0)
    def _():
        gain_out[...] = jnp.zeros_like(gain_out)

    cos, sin = cos_ref[...], -sin_ref[...]

    def back(grad, value, gain):
        scale = lax.rsqrt(jnp.mean(value * value, axis=-1, keepdims=True) + EPS)
        unit = value * scale
        turned = turn(grad, cos, sin)
        scaled = turned * gain
        result = scale * (scaled - unit * jnp.mean(scaled * unit, axis=-1, keepdims=True))
        return result.astype(BF16), jnp.sum(turned * unit, axis=0, keepdims=True)

    def columns(h):
        return slice(h * HEAD, (h + 1) * HEAD)

    q_total = jnp.zeros((1, HEAD), F32)
    k_total = jnp.zeros((1, HEAD), F32)
    per = q_heads // groups
    for h in range(q_heads):
        grad = dq_refs[h // per][:, columns(h % per)]
        a_out[:, columns(h)], more = back(grad, a_ref[:, columns(h)], head_ref[2:3, :])
        q_total += more
    tail = dlog_refs[0][...]
    for ref in dlog_refs[1:]:
        tail = tail + ref[...]
    a_out[:, q_heads * HEAD :] = tail
    per = k_heads // groups

    def total(h, first):
        found = dkv_refs[3 * (h // per) : 3 * (h // per) + 3]
        return sum(ref[:, columns(first + h % per)].astype(F32) for ref in found)

    for h in range(k_heads):
        b_out[:, columns(h)], more = back(total(h, 0), b_ref[:, columns(h)], head_ref[3:4, :])
        k_total += more
        b_out[:, columns(k_heads + h)] = total(h, per).astype(BF16)
    gain_out[0:1, :] += q_total
    gain_out[1:2, :] += k_total


def heads_back(tiles, tile, dqs, dkvs, dlogs, raw_a, raw_b, cos, sin, head, q_heads, k_heads):
    rows = raw_a.shape[0]
    groups = len(dqs)

    def at(width):
        return pl.BlockSpec((tile, width), lambda i, tiles: (i, 0))

    moved = pl.BlockSpec((tile, 2 * k_heads * HEAD // groups), lambda i, tiles: (tiles[i], 0))
    return pl.pallas_call(
        functools.partial(heads_back_kernel, q_heads, k_heads, groups),
        grid_spec=pltpu.PrefetchScalarGridSpec(
            num_scalar_prefetch=1,
            grid=(rows // tile,),
            in_specs=[at(q_heads * HEAD // groups)] * groups
            + [moved] * (3 * groups)
            + [at(LANES)] * groups
            + [at(raw_a.shape[1]), at(raw_b.shape[1]), at(HEAD), at(HEAD), fixed(head.shape)],
            out_specs=[
                at(raw_a.shape[1]),
                at(raw_b.shape[1]),
                pl.BlockSpec((8, HEAD), lambda i, tiles: (0, 0)),
            ],
        ),
        out_shape=[
            shaped(raw_a.shape, BF16),
            shaped(raw_b.shape, BF16),
            shaped((8, HEAD), F32),
        ],
        compiler_params=params(),
        cost_estimate=cost(rows * (q_heads + k_heads) * HEAD * 30, rows * 2000 * 16),
        name="heads_back",
    )(tiles, *dqs, *[x for group in dkvs for x in group], *dlogs, raw_a, raw_b, cos, sin, head)


def load_keys(kv_refs, kv_all, sem, block_rows, columns):
    copies = [
        pltpu.make_async_copy(
            ref.at[:, pl.ds(source, width)],
            kv_all.at[pl.ds(m * block_rows, block_rows), pl.ds(target, width)],
            sem.at[m, k],
        )
        for m, ref in enumerate(kv_refs)
        for k, (source, target, width) in enumerate(columns)
    ]
    for copy in copies:
        copy.start()
    for copy in copies:
        copy.wait()


def key_columns(k_heads, k_first, mine):
    return [
        (k_first * HEAD, 0, mine * HEAD),
        ((k_heads + k_first) * HEAD, mine * HEAD, mine * HEAD),
    ]


def turn_blocks(kv_all, turned, first, mine):
    @pl.loop(0, kv_all.shape[0] // KEY_TILE)
    def _(t):
        rows = pl.ds(pl.multiple_of(t * KEY_TILE, KEY_TILE), KEY_TILE)
        for g in range(mine):
            here = slice((first + g) * HEAD, (first + g + 1) * HEAD)
            turned[g, :, rows] = jnp.transpose(kv_all[rows, here])


def attend_kernel(k_heads, k_first, blocks, flags_ref, *refs):
    q_ref, bias_ref, sg_ref = refs[:3]
    kv_refs = refs[3 : 3 + blocks]
    att_out, gated_out, lse_out = refs[3 + blocks : 6 + blocks]
    kv_all, v_turned, q_turned, acc, norm, sem = refs[6 + blocks :]
    mine = kv_all.shape[1] // (2 * HEAD)
    share = q_ref.shape[1] // (mine * HEAD)
    tile = q_ref.shape[0]
    step = pl.program_id(0)
    key_tiles = kv_all.shape[0] // KEY_TILE

    @pl.when(step == 0)
    def _():
        block_rows = kv_all.shape[0] // blocks
        load_keys(kv_refs, kv_all, sem, block_rows, key_columns(k_heads, k_first, mine))
        turn_blocks(kv_all, v_turned, mine, mine)
        lse_out[...] = jnp.zeros_like(lse_out)

    for h in range(mine * share):
        g, j = h // share, h % share
        q_turned[g, :, j * tile : (j + 1) * tile] = jnp.transpose(
            q_ref[:, h * HEAD : (h + 1) * HEAD]
        )
    acc[...] = jnp.zeros_like(acc)
    norm[...] = jnp.zeros_like(norm)

    @pl.loop(0, key_tiles)
    def _(t):
        @pl.when(flags_ref[step * key_tiles + t] > 0)
        def _():
            rows = pl.ds(pl.multiple_of(t * KEY_TILE, KEY_TILE), KEY_TILE)
            bias = bias_ref[rows, :]
            bias = jnp.concatenate([bias] * share, axis=1)
            for first in range(0, mine, FORWARD_HEADS):
                found = range(first, min(first + FORWARD_HEADS, mine))
                scores = [
                    matmul(kv_all[rows, g * HEAD : (g + 1) * HEAD], q_turned[g]) for g in found
                ]
                weights = [jnp.exp2(score * (SCALE * LOG2E) + bias) for score in scores]
                parts = [
                    matmul(v_turned[g, :, rows], weight.astype(BF16))
                    for g, weight in zip(found, weights)
                ]
                sums = [
                    jnp.sum(weight.reshape(KEY_TILE // 8, 8, share * tile), axis=0)
                    for weight in weights
                ]
                for g, part, more in zip(found, parts, sums):
                    acc[g] += part
                    norm[g] += more

    for g in range(mine):
        total = jnp.sum(norm[g], axis=0, keepdims=True)
        attended = acc[g] / total
        log_total = jnp.log2(total)
        for j in range(share):
            h = g * share + j
            here = slice(h * HEAD, (h + 1) * HEAD)
            there = slice(j * tile, (j + 1) * tile)
            part = jnp.transpose(attended[:, there])
            att_out[:, here] = part
            q_head = k_first * share + h
            gated_out[:, here] = (part * sg_ref[:, q_head : q_head + 1]).astype(BF16)
            lse_out[h : h + 1, pl.ds(pl.multiple_of(step * tile, tile), tile)] = log_total[:, there]


def attend(flags, tile, queries, bias, sg, kvs, q_heads, k_heads, k_first, k_count):
    rows = queries.shape[0]
    blocks = len(kvs)
    keys = sum(kv.shape[0] for kv in kvs)
    share = q_heads // k_heads
    q_width, kv_width = k_count * share * HEAD, 2 * k_count * HEAD
    lse_rows = max(8, k_count * share)

    def at(width, column=0):
        return pl.BlockSpec((tile, width), lambda i, flags: (i, column))

    return pl.pallas_call(
        functools.partial(attend_kernel, k_heads, k_first, blocks),
        grid_spec=pltpu.PrefetchScalarGridSpec(
            num_scalar_prefetch=1,
            grid=(rows // tile,),
            in_specs=[
                at(q_width, k_first // k_count),
                pl.BlockSpec((None, keys, tile), lambda i, flags: (i, 0, 0)),
                at(LANES),
            ]
            + [pl.BlockSpec(memory_space=pl.ANY)] * blocks,
            out_specs=[
                at(q_width),
                at(q_width),
                pl.BlockSpec((lse_rows, rows), lambda i, flags: (0, 0)),
            ],
            scratch_shapes=[
                pltpu.VMEM((keys, kv_width), BF16),
                pltpu.VMEM((k_count, HEAD, keys), BF16),
                pltpu.VMEM((k_count, HEAD, share * tile), BF16),
                pltpu.VMEM((k_count, HEAD, share * tile), F32),
                pltpu.VMEM((k_count, 8, share * tile), F32),
                pltpu.SemaphoreType.DMA((blocks, 2)),
            ],
        ),
        out_shape=[
            shaped((rows, q_width), F32),
            shaped((rows, q_width), BF16),
            shaped((lse_rows, rows), F32),
        ],
        compiler_params=params(),
        cost_estimate=cost(
            2 * rows * keys * q_width * 2, rows * keys * 4, rows * keys * q_width // HEAD
        ),
        name="attend",
    )(flags, queries, bias, sg, *kvs)


def attend_back_kernel(k_heads, k_first, blocks, flags_ref, *refs):
    q_ref, dout_ref, bias_ref, lse_ref, delta_ref = refs[:5]
    kv_refs = refs[5 : 5 + blocks]
    dq_out, keep_out, send_out = refs[5 + blocks : 8 + blocks]
    kv_all, k_turned, dkv, q_rows, q_turned, d_rows, d_turned, dq, sem = refs[8 + blocks :]
    mine = kv_all.shape[1] // (2 * HEAD)
    share = q_ref.shape[1] // (mine * HEAD)
    tile = q_ref.shape[0]
    step = pl.program_id(0)
    key_tiles = kv_all.shape[0] // KEY_TILE

    @pl.when(step == 0)
    def _():
        block_rows = kv_all.shape[0] // blocks
        load_keys(kv_refs, kv_all, sem, block_rows, key_columns(k_heads, k_first, mine))
        turn_blocks(kv_all, k_turned, 0, mine)
        dkv[...] = jnp.zeros_like(dkv)

    dq[...] = jnp.zeros_like(dq)
    for h in range(mine * share):
        g, j = h // share, h % share
        here = slice(h * HEAD, (h + 1) * HEAD)
        there = slice(j * tile, (j + 1) * tile)
        q_rows[g, there] = q_ref[:, here]
        q_turned[g, :, there] = jnp.transpose(q_ref[:, here])
        d_rows[g, there] = dout_ref[:, here]
        d_turned[g, :, there] = jnp.transpose(dout_ref[:, here])

    q_first = k_first * share

    def row_of(ref, g, first):
        cut = first + g * share
        return jnp.concatenate([ref[cut + j : cut + j + 1, :] for j in range(share)], axis=1)

    @pl.loop(0, key_tiles)
    def _(t):
        @pl.when(flags_ref[step * key_tiles + t] > 0)
        def _():
            rows = pl.ds(pl.multiple_of(t * KEY_TILE, KEY_TILE), KEY_TILE)
            bias = bias_ref[rows, :]
            bias = jnp.concatenate([bias] * share, axis=1)
            for first in range(0, mine, BACKWARD_HEADS):
                found = range(first, min(first + BACKWARD_HEADS, mine))
                scores = [
                    matmul(kv_all[rows, g * HEAD : (g + 1) * HEAD], q_turned[g]) for g in found
                ]
                dprobs = [
                    matmul(kv_all[rows, (mine + g) * HEAD : (mine + g + 1) * HEAD], d_turned[g])
                    for g in found
                ]
                probs = [
                    jnp.exp2(score * (SCALE * LOG2E) + bias - row_of(lse_ref, g, q_first))
                    for g, score in zip(found, scores)
                ]
                dscores = [
                    (prob * (dprob - row_of(delta_ref, g, q_first))).astype(BF16)
                    for g, prob, dprob in zip(found, probs, dprobs)
                ]
                dvs = [matmul(prob.astype(BF16), d_rows[g]) for g, prob in zip(found, probs)]
                dks = [matmul(dscore, q_rows[g]) for g, dscore in zip(found, dscores)]
                dqs = [
                    matmul(k_turned[g, :, rows], dscore) for g, dscore in zip(found, dscores)
                ]
                for k, g in enumerate(found):
                    dkv[rows, (mine + g) * HEAD : (mine + g + 1) * HEAD] += dvs[k]
                    dkv[rows, g * HEAD : (g + 1) * HEAD] += dks[k]
                    dq[g] += dqs[k]

    for h in range(mine * share):
        g, j = h // share, h % share
        dq_out[:, h * HEAD : (h + 1) * HEAD] = jnp.transpose(
            dq[g, :, j * tile : (j + 1) * tile] * SCALE
        )

    @pl.when(step == pl.num_programs(0) - 1)
    def _():
        half = kv_all.shape[0] // 2
        k_all = slice(0, mine * HEAD)
        v_all = slice(mine * HEAD, 2 * mine * HEAD)
        for out, first in ((keep_out, 0), (send_out, half)):
            out[:, k_all] = (dkv[first : first + half, k_all] * SCALE).astype(BF16)
            out[:, v_all] = dkv[first : first + half, v_all].astype(BF16)


def attend_back(
    flags, tile, queries, dout, bias, lse, delta, kvs, q_heads, k_heads, k_first, k_count
):
    rows = queries.shape[0]
    blocks = len(kvs)
    keys = sum(kv.shape[0] for kv in kvs)
    share = q_heads // k_heads
    q_width, kv_width = k_count * share * HEAD, 2 * k_count * HEAD
    column = k_first // k_count

    def at(width, column=0):
        return pl.BlockSpec((tile, width), lambda i, flags: (i, column))

    whole = pl.BlockSpec((keys // 2, kv_width), lambda i, flags: (0, 0))

    def by_lane(array):
        return pl.BlockSpec((array.shape[0], tile), lambda i, flags: (0, i))

    return pl.pallas_call(
        functools.partial(attend_back_kernel, k_heads, k_first, blocks),
        grid_spec=pltpu.PrefetchScalarGridSpec(
            num_scalar_prefetch=1,
            grid=(rows // tile,),
            in_specs=[
                at(q_width, column),
                at(q_width, column),
                pl.BlockSpec((None, keys, tile), lambda i, flags: (i, 0, 0)),
                by_lane(lse),
                by_lane(delta),
            ]
            + [pl.BlockSpec(memory_space=pl.ANY)] * blocks,
            out_specs=[at(q_width), whole, whole],
            scratch_shapes=[
                pltpu.VMEM((keys, kv_width), BF16),
                pltpu.VMEM((k_count, HEAD, keys), BF16),
                pltpu.VMEM((keys, kv_width), F32),
                pltpu.VMEM((k_count, share * tile, HEAD), BF16),
                pltpu.VMEM((k_count, HEAD, share * tile), BF16),
                pltpu.VMEM((k_count, share * tile, HEAD), BF16),
                pltpu.VMEM((k_count, HEAD, share * tile), BF16),
                pltpu.VMEM((k_count, HEAD, share * tile), F32),
                pltpu.SemaphoreType.DMA((blocks, 2)),
            ],
        ),
        out_shape=[
            shaped((rows, q_width), F32),
            shaped((keys // 2, kv_width), BF16),
            shaped((keys // 2, kv_width), BF16),
        ],
        compiler_params=params(),
        cost_estimate=cost(
            2 * rows * keys * q_width * 5, rows * keys * 4, rows * keys * q_width // HEAD
        ),
        name="attend_back",
    )(flags, queries, dout, bias, lse, delta, *kvs)


def per_device(
    sizes,
    tokens,
    seg_ids,
    positions,
    cotangent,
    norm_in,
    norm_mid,
    query_gain,
    key_gain,
    query_weight,
    key_matrix,
    value_matrix,
    head_weight,
    out_weight,
    gate_weight,
    up_weight,
    down_weight,
):
    n_shard, n_ctx, n_tp = sizes
    ring = Ring(n_shard, n_ctx)
    row_count, width = tokens.shape
    block = query_weight.shape[0]
    q_width = query_weight.shape[1]
    k_width = key_matrix.shape[1]
    q_heads, k_heads = q_width // HEAD, k_width // HEAD
    chunk = gate_weight.shape[1] // CHUNKS
    rows = row_count // n_tp
    tile = row_tile(rows)
    n_head = head_weight.shape[1]
    gain_size = query_gain.shape[0]

    here_ctx = lax.axis_index("ctx")
    here_tp = lax.axis_index("tp")
    here = lax.axis_index("shard") * n_ctx + here_ctx
    order = lax.dynamic_index_in_dim(jnp.asarray(ring.order), here, keepdims=False)

    def row_tiles(size):
        ids = np.arange(row_count // size)
        per = rows // size
        return (((here_tp + ids // per) % n_tp) * per + ids % per).astype(jnp.int32)

    tiles = row_tiles(tile)

    def padded(gain):
        return jnp.pad(gain, (0, block - gain_size))[:, None]

    send_a = jnp.concatenate(
        [
            query_weight,
            head_weight,
            jnp.zeros((block, GAINS - n_head), BF16),
            norm_in[:, None],
            norm_mid[:, None],
            padded(query_gain),
            padded(key_gain),
            jnp.zeros((block, LANES - GAINS - 4), BF16),
        ],
        axis=1,
    )

    def chunk_block(j, *others):
        cut = slice(j * chunk, (j + 1) * chunk)
        gate, up, down = gate_weight[:, cut], up_weight[:, cut], down_weight[cut]
        gate, up, down = lax.optimization_barrier((gate, up, down, *others))[:3]
        return jnp.concatenate([gate, up, down.T], axis=1)

    ring_a = Gather(ring, send_a)
    ring_b = Gather(ring, jnp.concatenate([key_matrix, value_matrix], axis=1))

    def tick(others, *rings):
        for one in rings:
            one.step(*others)

    tick([], ring_a, ring_b)
    tok, cot, scale_in = enter(order, tiles, tile, tokens, cotangent)
    offset = here_ctx * row_count

    def own_rows(values):
        parts = [
            lax.dynamic_slice_in_dim(values, offset + ((here_tp + j) % n_tp) * rows, rows)
            for j in range(n_tp)
        ]
        return jnp.concatenate(parts)

    own_seg, own_pos = own_rows(seg_ids), own_rows(positions)
    block_order = sorted(range(n_ctx), key=lambda m: (m & 1, m))

    def key_rows(values):
        return jnp.concatenate(
            [
                lax.dynamic_slice_in_dim(values, (here_ctx ^ m) * row_count, row_count)
                for m in block_order
            ]
        )

    key_seg, key_pos = key_rows(seg_ids), key_rows(positions)
    tick([tok], ring_a, ring_b)
    half = HEAD // 2
    frequency = THETA ** (-(jnp.arange(half, dtype=F32) * 2.0) / HEAD)
    angles = own_pos.astype(F32)[:, None] * frequency[None, :]
    cos, sin = jnp.cos(angles), jnp.sin(angles)
    cos = jnp.concatenate([cos, cos], axis=1)
    sin = jnp.concatenate([-sin, sin], axis=1)
    tick([cos, sin], ring_a, ring_b)
    key_pos = hold(key_pos, cos)
    q_tiles, key_tiles = row_count // ROW_TILE, key_seg.shape[0] // KEY_TILE
    q_seg, q_pos = (v.reshape(q_tiles, 1, ROW_TILE) for v in (own_seg, own_pos))
    k_seg, k_pos = key_seg[None, :, None], key_pos[None, :, None]
    allowed = ((k_seg == 0) | (k_seg == q_seg)) & (k_pos <= q_pos)
    bias = jnp.where(allowed, 0.0, MASKED).astype(F32)
    tick([bias], ring_a, ring_b)
    flags = jnp.max(
        allowed.astype(jnp.int32).reshape(q_tiles, key_tiles, KEY_TILE, ROW_TILE), axis=(2, 3)
    ).reshape(-1)
    ring_o = Gather(ring, hold(out_weight.T, bias))
    tick([flags], ring_a, ring_b, ring_o)
    tick([], ring_a, ring_b, ring_o)
    ring_c = [Gather(ring, chunk_block(0, ring_o.last))]
    tick([], ring_a, ring_b, ring_o)
    ring_c.append(Gather(ring, chunk_block(1, ring_o.last)))
    tick([ring_a.last], ring_o, ring_c[0], ring_c[1])

    wide, head = gather_gains(order, ring_a.pieces, q_width)
    normed, raw_a, raw_b, queries, kv, sg = project(
        row_tiles(rows),
        rows,
        tok,
        scale_in,
        wide,
        head,
        cos,
        sin,
        ring_a.pieces,
        ring_b.pieces,
        q_heads,
        k_heads,
    )
    kvs = {0: kv}
    bit = n_ctx // 2
    while bit:
        for m in list(kvs):
            kvs[m | bit] = lax.ppermute(kvs[m], "ctx", [(i, i ^ bit) for i in range(n_ctx)])
        bit //= 2
    kvs = [kvs[m] for m in block_order]
    tick([queries], ring_o)
    cot_turned = flip([hold(cot, queries)], "flip_cot")
    ring_c.append(Gather(ring, chunk_block(2, cot_turned)))
    queries = hold(queries, cot_turned, ring_o.last)
    tick([kvs[-1]], ring_o, *ring_c)
    att, gated, lse = attend(
        flags, ROW_TILE, queries, bias, sg, kvs, q_heads, k_heads, 0, k_heads
    )
    while len(ring_o.pieces) < 2 * ring.length:
        tick([gated], ring_o)
    tick([gated], ring_c[0])
    own, sent = spread([(gated, ring_o.pieces, 0)], rows, "out_rows")
    arrived = tp_send(sent, rows, n_tp)
    tick([sent], *ring_c)
    reached = ring_c[0].last
    tick([], ring_c[0])
    own = hold(own, reached)
    middle, low = by_rows(
        middle_kernel, rows, tile, [own, tok], wide, arrived, [F32, BF16], "middle"
    )
    normed_mid = tp_gather(low, n_tp)
    tick([low], *ring_c)
    reached = ring_c[0].last
    tick([], *ring_c)
    normed_mid[0] = hold(normed_mid[0], reached)

    def units(j, *others):
        normed = [hold(normed_mid[0], *others)] + normed_mid[1:]
        return ff_units(normed, cot, ring_c[j].pieces, 0, chunk)

    def weight_grads(j, *others):
        hidden, dgate, dup = made[j]
        kept, sent = outer(
            [normed_turned, cot_turned],
            [hold(dgate, *others), dup, hidden],
            [0, 0, 1],
            "unit_grads",
        )
        return Reduce(ring, kept, sent)

    def mid_terms(j):
        return [
            (made[j][1], ring_c[j].pieces, 0),
            (made[j][2], ring_c[j].pieces, chunk),
        ]

    for _ in range(2 * ring.length):
        if len(ring_c[0].pieces) < 2 * ring.length:
            ring_c[0].step()
    made = [units(0)]
    tick([made[0][0]], ring_c[1], ring_c[2])
    normed_turned = flip([hold(normed_mid[0], made[0][0])] + normed_mid[1:], "flip_mid")
    sums_c = [weight_grads(0)]
    tick([sums_c[0].kept], ring_c[1], ring_c[2])
    while len(ring_c[1].pieces) < 2 * ring.length:
        tick([], ring_c[1], ring_c[2])
    made.append(units(1, sums_c[0].kept))
    tick([made[1][0]], ring_c[2], sums_c[0])
    start = spread(mid_terms(0) + mid_terms(1), rows, "mid_start", split=False)[0]
    tick([start], ring_c[2], sums_c[0])
    while len(ring_c[2].pieces) < 2 * ring.length:
        tick([], ring_c[2])
    made.append(units(2, start))
    tick([made[2][0]], sums_c[0])
    own, sent = spread(mid_terms(2), rows, "mid_rows", start=start)
    arrived = tp_send(sent, rows, n_tp)
    tick([sent], sums_c[0])
    sums_c.append(weight_grads(1, sent))
    tick([sums_c[1].kept], sums_c[0])
    sums_c.append(weight_grads(2, sums_c[1].kept))
    tick([sums_c[2].kept], *sums_c[:2])
    own = hold(own, sums_c[2].kept)
    dmid, low = by_rows(
        middle_back_kernel,
        rows,
        tile,
        [own, cot, middle],
        wide,
        arrived,
        [F32, BF16],
        "middle_back",
    )
    dmid_low = tp_gather(low, n_tp)
    tick([low], *sums_c)
    terms = [(hold(made[j][0], low), ring_c[j].pieces, 2 * chunk) for j in range(CHUNKS)]
    mixed_own, mixed_sent = spread(terms, rows, "mixed_rows")
    tick([mixed_own], *sums_c)
    mixed_sent = hold(mixed_sent, dmid_low[-1])
    mixed_arrived = tp_send(mixed_sent, rows, n_tp)
    dmid_low[0] = hold(dmid_low[0], mixed_own)

    dout, delta, dlog = attended_back(dmid_low, ring_o.pieces, att, sg)
    tick([dout], *sums_c)
    dq, keep, sent = attend_back(
        flags, ROW_TILE, queries, dout, bias, lse, delta, kvs, q_heads, k_heads, 0, k_heads
    )
    other = ring.swap(sent)
    extra = None
    for k in range(1, n_ctx // 2):
        piece = slice(k * row_count, (k + 1) * row_count)
        away = (keep[piece].astype(F32) + other[piece].astype(F32)).astype(BF16)
        m = block_order[k]
        came = lax.ppermute(away, "ctx", [(i, i ^ m) for i in range(n_ctx)])
        extra = came if extra is None else (extra.astype(F32) + came.astype(F32)).astype(BF16)
    tick([dq], *sums_c)
    dmid_low[0] = hold(dmid_low[0], dq)
    dmid_turned = flip(dmid_low, "flip_dmid")
    sum_o = Reduce(ring, *outer([dmid_turned], [hold(gated, dmid_turned)], [0], "out_grad"))
    normed_in_turned = flip([hold(normed, sum_o.kept)], "flip_in")
    output = by_rows(
        output_kernel,
        rows,
        tile,
        [hold(mixed_own, normed_in_turned), middle],
        None,
        mixed_arrived,
        [BF16],
        "output",
    )[0]
    output_parts = tp_gather(output, n_tp)
    tick([output], sum_o, *sums_c)
    dq = hold(dq, output)
    d_a, d_b, gain_sums = heads_back(
        tiles, tile, [dq], [[keep, other, extra]], [dlog], raw_a, raw_b, cos, sin, head, q_heads, k_heads
    )
    tick([d_a], sum_o, *sums_c)
    sum_a = Reduce(
        ring,
        *outer(
            [normed_in_turned],
            [d_a],
            [0],
            "query_grad",
            gains=(order, gain_sums),
            gained=q_width,
        ),
    )
    tick([sum_a.kept], sum_o)
    sum_b = Reduce(ring, *outer([normed_in_turned], [hold(d_b, sum_a.kept)], [0], "key_grad"))
    tick([sum_b.kept], sum_a, sum_o, *sums_c)
    own, sent = spread(
        [(hold(d_a, sum_b.kept), ring_a.pieces, 0), (d_b, ring_b.pieces, 0)], rows, "in_rows"
    )
    arrived = tp_send(sent, rows, n_tp)
    tick([sent], sum_a, sum_b, sum_o, *sums_c)
    tick([], sum_a, sum_b, sum_o)
    own = hold(own, sum_a.total, sum_b.total)
    tick([], sum_a, sum_b, sum_o)
    low = by_rows(
        input_back_kernel,
        rows,
        tile,
        [own, tok, scale_in, dmid],
        wide,
        arrived,
        [BF16],
        "input_back",
    )[0]
    parts = tp_gather(low, n_tp)
    tick([low], sum_a, sum_b, sum_o, *sums_c)
    output = leave(
        order, tiles, tile, [hold(output_parts[0], low)] + output_parts[1:], BF16, "leave_output"
    )
    for _ in range(2):
        tick([], sum_a, sum_b, sum_o)
    parts[0] = hold(parts[0], output, sum_a.total, sum_b.total)
    input_grad = leave(order, tiles, tile, parts, F32, "leave_grad")

    sums_c = [part.finish() for part in sums_c]
    sum_a, sum_b, sum_o = sum_a.finish(), sum_b.finish(), sum_o.finish()
    sum_gate = jnp.concatenate([part[:, :chunk] for part in sums_c], axis=1)
    sum_up = jnp.concatenate([part[:, chunk : 2 * chunk] for part in sums_c], axis=1)
    sum_down = jnp.concatenate([part[:, 2 * chunk :].T for part in sums_c], axis=0)
    mid_share = jnp.sum(sum_gate * gate_weight.astype(F32), axis=1) + jnp.sum(
        sum_up * up_weight.astype(F32), axis=1
    )
    in_share = (
        jnp.sum(sum_a[:, :q_width] * query_weight.astype(F32), axis=1)
        + jnp.sum(sum_b[:, :k_width] * key_matrix.astype(F32), axis=1)
        + jnp.sum(sum_b[:, k_width:] * value_matrix.astype(F32), axis=1)
        + jnp.sum(sum_a[:, q_width : q_width + n_head] * head_weight.astype(F32), axis=1)
    )
    small = jnp.stack(
        [
            in_share / norm_in.astype(F32),
            mid_share / norm_mid.astype(F32),
            sum_a[:, q_width + GAINS + 2],
            sum_a[:, q_width + GAINS + 3],
        ]
    )
    small = tp_total(small, n_tp)
    return (
        output,
        input_grad,
        small[0],
        small[1],
        small[2, :gain_size],
        small[3, :gain_size],
        sum_a[:, :q_width],
        sum_b[:, :k_width],
        sum_b[:, k_width:],
        sum_a[:, q_width : q_width + n_head],
        sum_o.T,
        sum_gate,
        sum_up,
        sum_down,
    )


def solution(mesh):
    sizes = (mesh.shape["shard"], mesh.shape["ctx"], mesh.shape["tp"])
    split = ("shard", "ctx")
    rows = P(split, None)
    vector = P(split)
    weight = P(split, "tp")
    turned = P("tp", split)
    return jax.shard_map(
        functools.partial(per_device, sizes),
        mesh=mesh,
        in_specs=(rows, P("shard"), P("shard"), rows)
        + (vector,) * 4
        + (weight,) * 4
        + (turned, weight, weight, turned),
        out_specs=(rows, rows) + (vector,) * 4 + (weight,) * 4 + (turned, weight, weight, turned),
        check_vma=False,
    )
```

```python
import functools

import jax
import jax.numpy as jnp
import numpy as np
from jax import lax
from jax.experimental import pallas as pl
from jax.experimental.pallas import tpu as pltpu
from jax.sharding import PartitionSpec as P

HEAD = 128
LANES = 128
EPS = 1e-06
THETA = 1000000.0
MASKED = -1e30
LOG2E = 1.4426950408889634
SCALE = HEAD ** (-0.5)
KEY_TILE = 256
CHUNKS = 3
COLUMN_TILE = 256
LAG = 3
ROW_TILE = 128
FORWARD_HEADS = 4
BACKWARD_HEADS = 2
GAINS = 64

F32 = jnp.float32
BF16 = jnp.bfloat16


def matmul(a, b, dims=((1,), (0,))):
    return lax.dot_general(a, b, (dims, ((), ())), preferred_element_type=F32)


def ring_tables(n_shard, n_ctx):
    path = []
    for x in range(n_ctx // 2):
        column = range(n_shard) if x % 2 == 0 else reversed(range(n_shard))
        path += [(z, x) for z in column]
    length = len(path)

    def device(place, core):
        z, x = path[place % length]
        return z * n_ctx + x * 2 + core

    hops = [(device(r, 0), device(r + 1, 0)) for r in range(length)]
    hops += [(device(r, 1), device(r - 1, 1)) for r in range(length)]
    order = np.zeros((n_shard * n_ctx, 2 * length), np.int32)
    for r in range(length):
        for core in (0, 1):
            back = -1 if core == 0 else 1
            order[device(r, core), 0::2] = [device(r + back * s, core) for s in range(length)]
            order[device(r, core), 1::2] = [device(r - back * s, 1 - core) for s in range(length)]
    return hops, order, length


def hold(value, *others):
    others = [other for other in others if other is not None]
    return lax.optimization_barrier((value, *others))[0] if others else value


class Ring:
    def __init__(self, n_shard, n_ctx):
        self.hops, self.order, self.length = ring_tables(n_shard, n_ctx)
        self.swaps = [(i, i ^ 1) for i in range(n_ctx)]

    def hop(self, value):
        return lax.ppermute(value, ("shard", "ctx"), self.hops)

    def swap(self, value):
        return lax.ppermute(value, "ctx", self.swaps)


class Gather:
    def __init__(self, ring, block):
        self.ring = ring
        self.last = block
        self.pieces = [block, ring.swap(block)]

    def done(self):
        return len(self.pieces) == 2 * self.ring.length

    def step(self, *others):
        if not self.done():
            self.last = self.ring.hop(hold(self.last, *others))
            self.pieces += [self.last, self.ring.swap(self.last)]
        return self.last


class Reduce:
    def __init__(self, ring, kept, sent):
        self.ring = ring
        self.rows = kept.shape[0] // ring.length
        self.kept = kept
        self.other = ring.swap(sent)
        self.place = 1
        self.total = self.own().astype(BF16)

    def own(self):
        first = (self.place % self.ring.length) * self.rows
        here = slice(first, first + self.rows)
        return self.kept[here].astype(F32) + self.other[here].astype(F32)

    def done(self):
        return self.place == self.ring.length

    def step(self, *others):
        if not self.done():
            self.place += 1
            total = self.ring.hop(hold(self.total, *others)).astype(F32) + self.own()
            self.total = total if self.place == self.ring.length else total.astype(BF16)
        return self.total

    def finish(self):
        while self.place < self.ring.length:
            self.step()
        return self.total


class Clock:
    def __init__(self):
        self.ticks = [[]]

    def tick(self, others, *rings):
        self.ticks.append([one.step(*others) for one in rings if not one.done()])

    def start(self, reduce):
        self.ticks[-1].append(reduce.other)
        return reduce

    def gate(self, value, lag=LAG):
        return hold(value, *[x for tick in self.ticks[:-lag][-3:] for x in tick])


def tp_send(sent, rows, n_tp):
    return [
        lax.ppermute(
            sent[(j - 1) * rows : j * rows], "tp", [(i, (i + j) % n_tp) for i in range(n_tp)]
        )
        for j in range(1, n_tp)
    ]


def tp_gather(block, n_tp):
    blocks = [block]
    for j in range(1, n_tp):
        blocks.append(lax.ppermute(block, "tp", [(i, (i - j) % n_tp) for i in range(n_tp)]))
    return blocks


def tp_total(value, n_tp):
    total = value
    for j in range(1, n_tp):
        total = total + lax.ppermute(value, "tp", [(i, (i + j) % n_tp) for i in range(n_tp)])
    return total


def row_tile(rows):
    return next(tile for tile in (128, 96, 64, 48, 32, 16) if rows % tile == 0)


def params(mib=56):
    return pltpu.CompilerParams(vmem_limit_bytes=mib << 20)


def cost(flops, moved, transcendentals=0):
    return pl.CostEstimate(
        flops=5 * flops, bytes_accessed=5 * moved, transcendentals=transcendentals
    )


def fixed(shape):
    return pl.BlockSpec(shape, lambda *_: (0,) * len(shape), pipeline_mode=pl.Buffered(1))


def shaped(shape, dtype):
    return jax.ShapeDtypeStruct(shape, dtype)


def enter_kernel(order_ref, rows_ref, tok_ref, cot_ref, tok_out, cot_out, scale_out):
    value = tok_ref[...].astype(F32)
    scale = lax.rsqrt(jnp.mean(value * value, axis=-1, keepdims=True) + EPS)
    scale_out[...] = jnp.broadcast_to(scale, scale_out.shape)
    for j in range(tok_ref.shape[1] // LANES):
        source = pl.multiple_of(order_ref[j] * LANES, LANES)
        here = slice(j * LANES, (j + 1) * LANES)
        tok_out[:, here] = tok_ref[:, pl.ds(source, LANES)]
        cot_out[:, here] = cot_ref[:, pl.ds(source, LANES)]


def enter(order, tiles, tile, tokens, cotangent):
    rows, width = tokens.shape
    block = pl.BlockSpec((tile, width), lambda i, order, tiles: (tiles[i], 0))
    out = pl.BlockSpec((tile, width), lambda i, order, tiles: (i, 0))
    return pl.pallas_call(
        enter_kernel,
        grid_spec=pltpu.PrefetchScalarGridSpec(
            num_scalar_prefetch=2,
            grid=(rows // tile,),
            in_specs=[block, block],
            out_specs=[out, out, pl.BlockSpec((tile, LANES), lambda i, order, tiles: (i, 0))],
        ),
        out_shape=[
            shaped((rows, width), BF16),
            shaped((rows, width), BF16),
            shaped((rows, LANES), F32),
        ],
        compiler_params=params(),
        cost_estimate=cost(rows * width * 4, rows * width * 8),
        name="enter",
    )(order, tiles, tokens, cotangent)


def leave_kernel(parts, order_ref, tiles_ref, *refs):
    out_ref = refs[parts]
    per = pl.num_programs(0) // parts
    for k in range(parts):

        @pl.when(pl.program_id(0) // per == k)
        def _():
            for j in range(out_ref.shape[1] // LANES):
                target = pl.multiple_of(order_ref[j] * LANES, LANES)
                out_ref[:, pl.ds(target, LANES)] = refs[k][
                    :, j * LANES : (j + 1) * LANES
                ].astype(out_ref.dtype)


def leave(order, tiles, tile, parts, dtype, name):
    rows, width = parts[0].shape
    per = rows // tile
    total = rows * len(parts)

    def part(k):
        return pl.BlockSpec(
            (tile, width), lambda i, order, tiles: (jnp.clip(i - k * per, 0, per - 1), 0)
        )

    return pl.pallas_call(
        functools.partial(leave_kernel, len(parts)),
        grid_spec=pltpu.PrefetchScalarGridSpec(
            num_scalar_prefetch=2,
            grid=(total // tile,),
            in_specs=[part(k) for k in range(len(parts))],
            out_specs=pl.BlockSpec((tile, width), lambda i, order, tiles: (tiles[i], 0)),
        ),
        out_shape=shaped((total, width), dtype),
        compiler_params=params(),
        cost_estimate=cost(0, total * width * 6),
        name=name,
    )(order, tiles, *parts)


def gains_kernel(order_ref, *refs):
    pieces, (wide_out, head_out) = refs[:-2], refs[-2:]
    size = HEAD // len(pieces)
    total = jnp.zeros((8, HEAD), F32)
    for j, piece in enumerate(pieces):
        turned = jnp.transpose(piece[...].astype(F32))[GAINS : GAINS + 8]
        wide_out[:, j * LANES : (j + 1) * LANES] = turned
        total += pltpu.roll(turned, order_ref[j] * size, 1)
    head_out[...] = total


def gather_gains(order, pieces, q_width):
    count = len(pieces)
    block = pieces[0].shape[0]
    spec = pl.BlockSpec((block, LANES), lambda i, order: (0, q_width // LANES))
    return pl.pallas_call(
        gains_kernel,
        grid_spec=pltpu.PrefetchScalarGridSpec(
            num_scalar_prefetch=1,
            grid=(1,),
            in_specs=[spec] * count,
            out_specs=[
                pl.BlockSpec((8, block * count), lambda i, order: (0, 0)),
                pl.BlockSpec((8, HEAD), lambda i, order: (0, 0)),
            ],
        ),
        out_shape=[shaped((8, block * count), F32), shaped((8, HEAD), F32)],
        compiler_params=params(),
        cost_estimate=cost(0, block * count * LANES * 2),
        name="gather_gains",
    )(order, *pieces)


def turn(value, cos, sin):
    return value * cos + pltpu.roll(value, HEAD // 2, 1) * sin


def project_kernel(q_heads, k_heads, count, tiles_ref, *refs):
    tok_ref, scale_ref, wide_ref, head_ref, cos_ref, sin_ref = refs[:6]
    a_refs, b_refs = refs[6 : 6 + count], refs[6 + count : 6 + 2 * count]
    normed_out, a_out, b_out, q_out, kv_out, sg_out = refs[6 + 2 * count :]
    cos, sin = cos_ref[...], sin_ref[...]
    normed = (tok_ref[...].astype(F32) * scale_ref[:, :1] * wide_ref[0:1, :]).astype(BF16)
    normed_out[...] = normed

    def rotated(value, gain):
        scale = lax.rsqrt(jnp.mean(value * value, axis=-1, keepdims=True) + EPS)
        return turn(value * scale * gain, cos, sin).astype(BF16)

    def product(refs, here):
        return matmul(normed_out[...], jnp.concatenate([ref[:, here] for ref in refs], axis=0))

    q_width, k_width = q_heads * HEAD, k_heads * HEAD
    q_tile, k_tile = min(COLUMN_TILE, q_width), min(COLUMN_TILE, k_width)

    @pl.loop(0, q_width // q_tile, unroll=True)
    def _(i):
        here = pl.ds(pl.multiple_of(i * q_tile, q_tile), q_tile)
        value = product(a_refs, here)
        a_out[:, here] = value
        q_out[:, here] = jnp.concatenate(
            [
                rotated(value[:, h * HEAD : (h + 1) * HEAD], head_ref[2:3, :])
                for h in range(q_tile // HEAD)
            ],
            axis=1,
        )

    tail = slice(q_width, q_width + LANES)
    value = product(a_refs, tail)
    a_out[:, tail] = value
    sg_out[...] = jax.nn.sigmoid(value)

    @pl.loop(0, k_width // k_tile, unroll=True)
    def _(i):
        here = pl.ds(pl.multiple_of(i * k_tile, k_tile), k_tile)
        value = product(b_refs, here)
        b_out[:, here] = value
        kv_out[:, here] = jnp.concatenate(
            [
                rotated(value[:, h * HEAD : (h + 1) * HEAD], head_ref[3:4, :])
                for h in range(k_tile // HEAD)
            ],
            axis=1,
        )

    @pl.loop(0, k_width // k_tile, unroll=True)
    def _(i):
        here = pl.ds(pl.multiple_of(k_width + i * k_tile, k_tile), k_tile)
        value = product(b_refs, here)
        b_out[:, here] = value
        kv_out[:, here] = value.astype(BF16)


def project(tiles, tile, tok, scale, wide, head, cos, sin, pieces_a, pieces_b, q_heads, k_heads):
    rows, width = tok.shape
    count = len(pieces_a)
    a_width, b_width = pieces_a[0].shape[1], pieces_b[0].shape[1]

    def at(width):
        return pl.BlockSpec((tile, width), lambda i, tiles: (i, 0))

    return pl.pallas_call(
        functools.partial(project_kernel, q_heads, k_heads, count),
        grid_spec=pltpu.PrefetchScalarGridSpec(
            num_scalar_prefetch=1,
            grid=(rows // tile,),
            in_specs=[at(width), at(LANES), fixed(wide.shape), fixed(head.shape), at(HEAD), at(HEAD)]
            + [fixed(piece.shape) for piece in pieces_a + pieces_b],
            out_specs=[
                at(width),
                at(a_width),
                at(b_width),
                at(q_heads * HEAD),
                pl.BlockSpec((tile, 2 * k_heads * HEAD), lambda i, tiles: (tiles[i], 0)),
                at(LANES),
            ],
        ),
        out_shape=[
            shaped((rows, width), BF16),
            shaped((rows, a_width), F32),
            shaped((rows, b_width), F32),
            shaped((rows, q_heads * HEAD), BF16),
            shaped((rows, 2 * k_heads * HEAD), BF16),
            shaped((rows, LANES), F32),
        ],
        compiler_params=params(),
        cost_estimate=cost(
            2 * rows * width * (a_width + b_width), width * (a_width + b_width) * 2 + rows * width * 16
        ),
        name="project",
    )(tiles, tok, scale, wide, head, cos, sin, *pieces_a, *pieces_b)


def spread_kernel(terms, count, rows, has_start, split, *refs):
    used = 0
    groups = []
    for width, _ in terms:
        groups.append((refs[used], refs[used + 1 : used + 1 + count]))
        used += 1 + count
    start_ref = None
    if has_start:
        start_ref = refs[used]
        used += 1
    outs = 2 if split else 1
    out_refs, scratch = refs[used : used + outs], refs[used + outs :]
    bufs, sem = scratch[:-1], scratch[-1]
    step = pl.program_id(0)
    block = groups[0][1][0].shape[0]

    def copies(s):
        slot = s % 2
        found = []
        for t, (width, offset) in enumerate(terms):
            for k in range(2):
                found.append(
                    pltpu.make_async_copy(
                        groups[t][1][2 * s + k].at[:, pl.ds(offset, width)],
                        bufs[t].at[slot, pl.ds(k * block, block)],
                        sem.at[slot, 2 * t + k],
                    )
                )
        return found

    for s in range(count // 2):

        @pl.when(step == s)
        def _():
            if s == 0:
                for copy in copies(0):
                    copy.start()
            if s + 1 < count // 2:
                for copy in copies(s + 1):
                    copy.start()
            for copy in copies(s):
                copy.wait()

    slot = lax.rem(step, 2)
    total = None
    for t in range(len(terms)):
        part = matmul(groups[t][0][...], bufs[t][slot], ((1,), (1,)))
        total = part if total is None else total + part
    if has_start:
        total = total + start_ref[...]
    if split:
        out_refs[0][...] = total[:rows]
        out_refs[1][...] = total[rows:].astype(BF16)
    else:
        out_refs[0][...] = total


def spread(terms, rows, name, start=None, split=True):
    count = len(terms[0][1])
    block = terms[0][1][0].shape[0]
    total = terms[0][0].shape[0]
    width = block * count
    sizes = [(x.shape[1], offset) for x, _, offset in terms]
    operands, specs = [], []
    for x, pieces, _ in terms:
        operands += [x, *pieces]
        specs += [fixed(x.shape)] + [pl.BlockSpec(memory_space=pl.ANY)] * count
    column = pl.BlockSpec((total, 2 * block), lambda s: (0, s))
    if start is not None:
        operands.append(start)
        specs.append(column)
    if split:
        out_specs = [
            pl.BlockSpec((rows, 2 * block), lambda s: (0, s)),
            pl.BlockSpec((total - rows, 2 * block), lambda s: (0, s)),
        ]
        out_shape = [shaped((rows, width), F32), shaped((total - rows, width), BF16)]
    else:
        out_specs, out_shape = [column], [shaped((total, width), F32)]
    depth = sum(size for size, _ in sizes)
    return pl.pallas_call(
        functools.partial(spread_kernel, sizes, count, rows, start is not None, split),
        grid=(count // 2,),
        in_specs=specs,
        out_specs=out_specs,
        out_shape=out_shape,
        scratch_shapes=[pltpu.VMEM((2, 2 * block, size), BF16) for size, _ in sizes]
        + [pltpu.SemaphoreType.DMA((2, 2 * len(sizes)))],
        compiler_params=params(),
        cost_estimate=cost(2 * total * depth * width, depth * width * 2 + total * width * 6),
        name=name,
    )(*operands)


def units_kernel(parts, count, *refs):
    n_refs, c_ref = refs[:parts], refs[parts]
    weights = refs[parts + 1 : parts + 1 + 3 * count]
    hid_out, dgate_out, dup_out = refs[parts + 1 + 3 * count :]

    def weight(k):
        return jnp.concatenate([ref[...] for ref in weights[k * count : (k + 1) * count]], axis=0)

    rows = n_refs[0].shape[0]
    w_gate, w_up, w_down = weight(0), weight(1), weight(2)
    for k in range(parts):
        here = slice(k * rows, (k + 1) * rows)
        gate = matmul(n_refs[k][...], w_gate)
        up = matmul(n_refs[k][...], w_up)
        dhid = matmul(c_ref[here], w_down)
        sig = jax.nn.sigmoid(gate)
        silu = gate * sig
        hid_out[here] = (silu * up).astype(BF16)
        dgate_out[here] = (dhid * up * sig * (1.0 + gate * (1.0 - sig))).astype(BF16)
        dup_out[here] = (dhid * silu).astype(BF16)


def ff_units(normed, cot, pieces, offset, chunk):
    rows, width = cot.shape
    count = len(pieces)
    block = pieces[0].shape[0]
    specs, operands = [], []
    for k in range(3):
        first = (offset + k * chunk) // COLUMN_TILE
        specs += [pl.BlockSpec((block, COLUMN_TILE), lambda i, first=first: (0, first + i))] * count
        operands += pieces
    out = pl.BlockSpec((rows, COLUMN_TILE), lambda i: (0, i))
    return pl.pallas_call(
        functools.partial(units_kernel, len(normed), count),
        grid=(chunk // COLUMN_TILE,),
        in_specs=[fixed(part.shape) for part in normed] + [fixed(cot.shape)] + specs,
        out_specs=[out] * 3,
        out_shape=[shaped((rows, chunk), BF16)] * 3,
        compiler_params=params(),
        cost_estimate=cost(
            6 * rows * width * chunk, 3 * width * chunk * 2 + rows * width * 4, rows * chunk
        ),
        name="ff_units",
    )(*normed, cot, *operands)


def attended_back_kernel(parts, count, *refs):
    weights = refs[parts : parts + count]
    att_ref, sg_ref = refs[parts + count : parts + count + 2]
    dout_out, delta_out, dlog_out, dgat = refs[parts + count + 2 :]
    step = pl.program_id(0)

    @pl.when(step == 0)
    def _():
        delta_out[...] = jnp.zeros_like(delta_out)
        dlog_out[...] = jnp.zeros_like(dlog_out)

    weight = jnp.concatenate([ref[...] for ref in weights], axis=0)
    rows = refs[0].shape[0]
    for k in range(parts):
        dgat[k * rows : (k + 1) * rows] = matmul(refs[k][...], weight)
    lane = lax.broadcasted_iota(jnp.int32, (ROW_TILE, LANES), 1)
    place = lax.broadcasted_iota(jnp.int32, (delta_out.shape[0], ROW_TILE), 0)
    for r in range(dgat.shape[0] // ROW_TILE):
        there = slice(r * ROW_TILE, (r + 1) * ROW_TILE)
        dlog = dlog_out[there].astype(F32)
        delta = delta_out[:, there]
        for j in range(COLUMN_TILE // HEAD):
            head = step * (COLUMN_TILE // HEAD) + j
            here = slice(j * HEAD, (j + 1) * HEAD)
            sg = jnp.sum(jnp.where(lane == head, sg_ref[there], 0.0), axis=1, keepdims=True)
            grad = dgat[there, here]
            att = att_ref[there, here]
            rounded = (grad * sg).astype(BF16)
            dout_out[there, here] = rounded
            turned = jnp.transpose(rounded.astype(F32) * att)
            delta = jnp.where(place == head, jnp.sum(turned, axis=0, keepdims=True), delta)
            dlog_h = jnp.sum(grad * att, axis=1, keepdims=True) * sg * (1.0 - sg)
            dlog = jnp.where(lane == head, dlog_h, dlog)
        dlog_out[there] = dlog.astype(BF16)
        delta_out[:, there] = delta


def attended_back(lefts, pieces, att, sg):
    count = len(pieces)
    block = pieces[0].shape[0]
    rows = lefts[0].shape[0] * len(lefts)
    width = att.shape[1]
    column = pl.BlockSpec((rows, COLUMN_TILE), lambda i: (0, i))
    delta_rows = max(8, width // HEAD)
    return pl.pallas_call(
        functools.partial(attended_back_kernel, len(lefts), count),
        grid=(width // COLUMN_TILE,),
        in_specs=[fixed(left.shape) for left in lefts]
        + [pl.BlockSpec((block, COLUMN_TILE), lambda i: (0, i))] * count
        + [column, fixed(sg.shape)],
        out_specs=[
            column,
            pl.BlockSpec((delta_rows, rows), lambda i: (0, 0)),
            pl.BlockSpec((rows, LANES), lambda i: (0, 0)),
        ],
        out_shape=[
            shaped((rows, width), BF16),
            shaped((delta_rows, rows), F32),
            shaped((rows, LANES), BF16),
        ],
        scratch_shapes=[pltpu.VMEM((rows, COLUMN_TILE), F32)],
        compiler_params=params(),
        cost_estimate=cost(2 * rows * block * count * width, block * count * width * 2 + rows * width * 10),
        name="attended_back",
    )(*lefts, *pieces, att, sg)


def flip_kernel(*refs):
    rows = refs[0].shape[0]
    for k, ref in enumerate(refs[:-1]):
        refs[-1][:, k * rows : (k + 1) * rows] = jnp.transpose(ref[...])


def flip(parts, name):
    rows, width = parts[0].shape
    return pl.pallas_call(
        flip_kernel,
        grid=(width // COLUMN_TILE,),
        in_specs=[pl.BlockSpec((rows, COLUMN_TILE), lambda i: (0, i))] * len(parts),
        out_specs=pl.BlockSpec((COLUMN_TILE, rows * len(parts)), lambda i: (i, 0)),
        out_shape=shaped((width, rows * len(parts)), BF16),
        compiler_params=params(),
        cost_estimate=cost(0, rows * width * len(parts) * 4),
        name=name,
    )(*parts)


def outer_kernel(which, steps, gained, *refs):
    used = 0
    order_ref = gain_ref = None
    if gained is not None:
        order_ref, gain_ref = refs[0], refs[1]
        used = 2
    n_left = max(which) + 1
    lefts = refs[used : used + n_left]
    rights = refs[used + n_left : used + n_left + len(which)]
    kept_out, sent_out = refs[used + n_left + len(which) :]
    step = pl.program_id(0)
    count = lefts[0].shape[0] // LANES
    for k, left in enumerate(which):

        @pl.when(step // steps == k)
        def _():
            for j in range(count // 2):
                there = slice(2 * j * LANES, (2 * j + 2) * LANES)
                total = matmul(lefts[left][there], rights[k][...]).astype(BF16)
                kept_out[j * LANES : (j + 1) * LANES] = total[:LANES]
                sent_out[j * LANES : (j + 1) * LANES] = total[LANES:]

    if gained is not None:
        size = HEAD // count
        lane = lax.broadcasted_iota(jnp.int32, (16, LANES), 1)
        row = lax.broadcasted_iota(jnp.int32, (16, LANES), 0)
        tile = kept_out.shape[1]

        @pl.when(step == gained // tile)
        def _():
            there = slice(gained % tile, gained % tile + LANES)
            for j in range(count):
                more = jnp.zeros((16, LANES), F32)
                for k in range(2):
                    sums = jnp.broadcast_to(gain_ref[k : k + 1, :], (16, LANES))
                    picked = (lane == order_ref[j] * size + row) & (row < size)
                    column = jnp.sum(jnp.where(picked, sums, 0.0), axis=1, keepdims=True)
                    more += jnp.where(lane == GAINS + 2 + k, column, 0.0)
                out = kept_out if j % 2 == 0 else sent_out
                here = slice((j // 2) * LANES, (j // 2) * LANES + 16)
                out[here, there] = (out[here, there].astype(F32) + more).astype(BF16)


def outer(lefts, rights, which, name, gains=None, gained=None):
    width, rows = lefts[0].shape
    size = rights[0].shape[1]
    tile = next(tile for tile in (384, 256, 128) if size % tile == 0)
    if len(rights) > 1:
        tile = COLUMN_TILE
    steps = size // tile
    specs, operands = [], []
    if gained is not None:
        operands += list(gains)
        specs += [pl.BlockSpec(memory_space=pltpu.SMEM), fixed(gains[1].shape)]
    operands += list(lefts) + list(rights)
    specs += [fixed(left.shape) for left in lefts]
    for k in range(len(rights)):
        specs.append(
            pl.BlockSpec((rows, tile), lambda i, k=k: (0, jnp.clip(i - k * steps, 0, steps - 1)))
        )
    total = size * len(rights)
    out = pl.BlockSpec((width // 2, tile), lambda i: (0, i))
    return pl.pallas_call(
        functools.partial(outer_kernel, which, steps, gained),
        grid=(steps * len(rights),),
        in_specs=specs,
        out_specs=[out, out],
        out_shape=[shaped((width // 2, total), BF16)] * 2,
        compiler_params=params(),
        cost_estimate=cost(2 * rows * width * total, width * total * 2 + rows * (width + total) * 2),
        name=name,
    )(*operands)


def arrived_sum(own_ref, refs):
    total = own_ref[...]
    for ref in refs:
        total = total + ref[...].astype(F32)
    return total


def mean_of(value):
    return jnp.mean(value, axis=-1, keepdims=True)


def middle_kernel(own_ref, tok_ref, wide_ref, *refs):
    middle_out, normed_out = refs[-2:]
    middle = tok_ref[...].astype(F32) + arrived_sum(own_ref, refs[:-2])
    middle_out[...] = middle
    scale = lax.rsqrt(mean_of(middle * middle) + EPS)
    normed_out[...] = (middle * scale * wide_ref[1:2, :]).astype(BF16)


def middle_back_kernel(own_ref, cot_ref, middle_ref, wide_ref, *refs):
    dmid_out, low_out = refs[-2:]
    middle = middle_ref[...]
    scale = lax.rsqrt(mean_of(middle * middle) + EPS)
    unit = middle * scale
    grad = arrived_sum(own_ref, refs[:-2]) * wide_ref[1:2, :]
    dmid = cot_ref[...].astype(F32) + scale * (grad - unit * mean_of(grad * unit))
    dmid_out[...] = dmid
    low_out[...] = dmid.astype(BF16)


def output_kernel(own_ref, middle_ref, *refs):
    refs[-1][...] = (middle_ref[...] + arrived_sum(own_ref, refs[:-1])).astype(BF16)


def input_back_kernel(own_ref, tok_ref, scale_ref, dmid_ref, wide_ref, *refs):
    scale = scale_ref[:, :1]
    unit = tok_ref[...].astype(F32) * scale
    grad = arrived_sum(own_ref, refs[:-1]) * wide_ref[0:1, :]
    refs[-1][...] = (dmid_ref[...] + scale * (grad - unit * mean_of(grad * unit))).astype(BF16)


def by_rows(kernel, rows, tile, operands, wide, arrived, dtypes, name):
    width = operands[0].shape[1]

    def at(operand):
        return pl.BlockSpec((tile, operand.shape[1]), lambda i: (i, 0))

    specs = [at(operand) for operand in operands]
    if wide is not None:
        specs.append(fixed(wide.shape))
        operands = operands + [wide]
    specs += [at(operand) for operand in arrived]
    out = pl.BlockSpec((tile, width), lambda i: (i, 0))
    return pl.pallas_call(
        kernel,
        grid=(rows // tile,),
        in_specs=specs,
        out_specs=[out] * len(dtypes),
        out_shape=[shaped((rows, width), dtype) for dtype in dtypes],
        compiler_params=params(),
        cost_estimate=cost(rows * width * 12, rows * width * 14),
        name=name,
    )(*operands, *arrived)


def heads_back_kernel(q_heads, k_heads, groups, tiles_ref, *refs):
    dq_refs = refs[:groups]
    dkv_refs = refs[groups : 4 * groups]
    dlog_refs = refs[4 * groups : 5 * groups]
    a_ref, b_ref, cos_ref, sin_ref, head_ref = refs[5 * groups : 5 * groups + 5]
    a_out, b_out, gain_out = refs[5 * groups + 5 :]

    @pl.when(pl.program_id(0) == 0)
    def _():
        gain_out[...] = jnp.zeros_like(gain_out)

    cos, sin = cos_ref[...], -sin_ref[...]

    def back(grad, value, gain):
        scale = lax.rsqrt(jnp.mean(value * value, axis=-1, keepdims=True) + EPS)
        unit = value * scale
        turned = turn(grad, cos, sin)
        scaled = turned * gain
        result = scale * (scaled - unit * jnp.mean(scaled * unit, axis=-1, keepdims=True))
        return result.astype(BF16), jnp.sum(turned * unit, axis=0, keepdims=True)

    def columns(h):
        return slice(h * HEAD, (h + 1) * HEAD)

    q_total = jnp.zeros((1, HEAD), F32)
    k_total = jnp.zeros((1, HEAD), F32)
    per = q_heads // groups
    for h in range(q_heads):
        grad = dq_refs[h // per][:, columns(h % per)]
        a_out[:, columns(h)], more = back(grad, a_ref[:, columns(h)], head_ref[2:3, :])
        q_total += more
    tail = dlog_refs[0][...]
    for ref in dlog_refs[1:]:
        tail = tail + ref[...]
    a_out[:, q_heads * HEAD :] = tail
    per = k_heads // groups

    def total(h, first):
        found = dkv_refs[3 * (h // per) : 3 * (h // per) + 3]
        return sum(ref[:, columns(first + h % per)].astype(F32) for ref in found)

    for h in range(k_heads):
        b_out[:, columns(h)], more = back(total(h, 0), b_ref[:, columns(h)], head_ref[3:4, :])
        k_total += more
        b_out[:, columns(k_heads + h)] = total(h, per).astype(BF16)
    gain_out[0:1, :] += q_total
    gain_out[1:2, :] += k_total


def heads_back(tiles, tile, dqs, dkvs, dlogs, raw_a, raw_b, cos, sin, head, q_heads, k_heads):
    rows = raw_a.shape[0]
    groups = len(dqs)

    def at(width):
        return pl.BlockSpec((tile, width), lambda i, tiles: (i, 0))

    moved = pl.BlockSpec((tile, 2 * k_heads * HEAD // groups), lambda i, tiles: (tiles[i], 0))
    return pl.pallas_call(
        functools.partial(heads_back_kernel, q_heads, k_heads, groups),
        grid_spec=pltpu.PrefetchScalarGridSpec(
            num_scalar_prefetch=1,
            grid=(rows // tile,),
            in_specs=[at(q_heads * HEAD // groups)] * groups
            + [moved] * (3 * groups)
            + [at(LANES)] * groups
            + [at(raw_a.shape[1]), at(raw_b.shape[1]), at(HEAD), at(HEAD), fixed(head.shape)],
            out_specs=[
                at(raw_a.shape[1]),
                at(raw_b.shape[1]),
                pl.BlockSpec((8, HEAD), lambda i, tiles: (0, 0)),
            ],
        ),
        out_shape=[
            shaped(raw_a.shape, BF16),
            shaped(raw_b.shape, BF16),
            shaped((8, HEAD), F32),
        ],
        compiler_params=params(),
        cost_estimate=cost(rows * (q_heads + k_heads) * HEAD * 30, rows * 2000 * 16),
        name="heads_back",
    )(tiles, *dqs, *[x for group in dkvs for x in group], *dlogs, raw_a, raw_b, cos, sin, head)


def load_keys(kv_refs, kv_all, sem, block_rows, columns):
    copies = [
        pltpu.make_async_copy(
            ref.at[:, pl.ds(source, width)],
            kv_all.at[pl.ds(m * block_rows, block_rows), pl.ds(target, width)],
            sem.at[m, k],
        )
        for m, ref in enumerate(kv_refs)
        for k, (source, target, width) in enumerate(columns)
    ]
    for copy in copies:
        copy.start()
    for copy in copies:
        copy.wait()


def key_columns(k_heads, k_first, mine):
    return [
        (k_first * HEAD, 0, mine * HEAD),
        ((k_heads + k_first) * HEAD, mine * HEAD, mine * HEAD),
    ]


def turn_blocks(kv_all, turned, first, mine):
    @pl.loop(0, kv_all.shape[0] // KEY_TILE)
    def _(t):
        rows = pl.ds(pl.multiple_of(t * KEY_TILE, KEY_TILE), KEY_TILE)
        for g in range(mine):
            here = slice((first + g) * HEAD, (first + g + 1) * HEAD)
            turned[g, :, rows] = jnp.transpose(kv_all[rows, here])


def attend_kernel(k_heads, k_first, blocks, flags_ref, *refs):
    q_ref, bias_ref, sg_ref = refs[:3]
    kv_refs = refs[3 : 3 + blocks]
    att_out, gated_out, lse_out = refs[3 + blocks : 6 + blocks]
    kv_all, v_turned, q_turned, acc, norm, sem = refs[6 + blocks :]
    mine = kv_all.shape[1] // (2 * HEAD)
    share = q_ref.shape[1] // (mine * HEAD)
    tile = q_ref.shape[0]
    step = pl.program_id(0)
    key_tiles = kv_all.shape[0] // KEY_TILE

    @pl.when(step == 0)
    def _():
        block_rows = kv_all.shape[0] // blocks
        load_keys(kv_refs, kv_all, sem, block_rows, key_columns(k_heads, k_first, mine))
        turn_blocks(kv_all, v_turned, mine, mine)
        lse_out[...] = jnp.zeros_like(lse_out)

    for h in range(mine * share):
        g, j = h // share, h % share
        q_turned[g, :, j * tile : (j + 1) * tile] = jnp.transpose(
            q_ref[:, h * HEAD : (h + 1) * HEAD]
        )
    acc[...] = jnp.zeros_like(acc)
    norm[...] = jnp.zeros_like(norm)

    @pl.loop(0, key_tiles)
    def _(t):
        @pl.when(flags_ref[step * key_tiles + t] > 0)
        def _():
            rows = pl.ds(pl.multiple_of(t * KEY_TILE, KEY_TILE), KEY_TILE)
            bias = bias_ref[rows, :]
            bias = jnp.concatenate([bias] * share, axis=1)
            for first in range(0, mine, FORWARD_HEADS):
                found = range(first, min(first + FORWARD_HEADS, mine))
                scores = [
                    matmul(kv_all[rows, g * HEAD : (g + 1) * HEAD], q_turned[g]) for g in found
                ]
                weights = [jnp.exp2(score * (SCALE * LOG2E) + bias) for score in scores]
                parts = [
                    matmul(v_turned[g, :, rows], weight.astype(BF16))
                    for g, weight in zip(found, weights)
                ]
                sums = [
                    jnp.sum(weight.reshape(KEY_TILE // 8, 8, share * tile), axis=0)
                    for weight in weights
                ]
                for g, part, more in zip(found, parts, sums):
                    acc[g] += part
                    norm[g] += more

    for g in range(mine):
        total = jnp.sum(norm[g], axis=0, keepdims=True)
        attended = acc[g] / total
        log_total = jnp.log2(total)
        for j in range(share):
            h = g * share + j
            here = slice(h * HEAD, (h + 1) * HEAD)
            there = slice(j * tile, (j + 1) * tile)
            part = jnp.transpose(attended[:, there])
            att_out[:, here] = part
            q_head = k_first * share + h
            gated_out[:, here] = (part * sg_ref[:, q_head : q_head + 1]).astype(BF16)
            lse_out[h : h + 1, pl.ds(pl.multiple_of(step * tile, tile), tile)] = log_total[:, there]


def attend(flags, tile, queries, bias, sg, kvs, q_heads, k_heads, k_first, k_count):
    rows = queries.shape[0]
    blocks = len(kvs)
    keys = sum(kv.shape[0] for kv in kvs)
    share = q_heads // k_heads
    q_width, kv_width = k_count * share * HEAD, 2 * k_count * HEAD
    lse_rows = max(8, k_count * share)

    def at(width, column=0):
        return pl.BlockSpec((tile, width), lambda i, flags: (i, column))

    return pl.pallas_call(
        functools.partial(attend_kernel, k_heads, k_first, blocks),
        grid_spec=pltpu.PrefetchScalarGridSpec(
            num_scalar_prefetch=1,
            grid=(rows // tile,),
            in_specs=[
                at(q_width, k_first // k_count),
                pl.BlockSpec((None, keys, tile), lambda i, flags: (i, 0, 0)),
                at(LANES),
            ]
            + [pl.BlockSpec(memory_space=pl.ANY)] * blocks,
            out_specs=[
                at(q_width),
                at(q_width),
                pl.BlockSpec((lse_rows, rows), lambda i, flags: (0, 0)),
            ],
            scratch_shapes=[
                pltpu.VMEM((keys, kv_width), BF16),
                pltpu.VMEM((k_count, HEAD, keys), BF16),
                pltpu.VMEM((k_count, HEAD, share * tile), BF16),
                pltpu.VMEM((k_count, HEAD, share * tile), F32),
                pltpu.VMEM((k_count, 8, share * tile), F32),
                pltpu.SemaphoreType.DMA((blocks, 2)),
            ],
        ),
        out_shape=[
            shaped((rows, q_width), F32),
            shaped((rows, q_width), BF16),
            shaped((lse_rows, rows), F32),
        ],
        compiler_params=params(),
        cost_estimate=cost(
            2 * rows * keys * q_width * 2, rows * keys * 4, rows * keys * q_width // HEAD
        ),
        name="attend",
    )(flags, queries, bias, sg, *kvs)


def attend_back_kernel(k_heads, k_first, blocks, flags_ref, *refs):
    q_ref, dout_ref, bias_ref, lse_ref, delta_ref = refs[:5]
    kv_refs = refs[5 : 5 + blocks]
    dq_out, keep_out, send_out = refs[5 + blocks : 8 + blocks]
    kv_all, k_turned, dkv, q_rows, q_turned, d_rows, d_turned, dq, sem = refs[8 + blocks :]
    mine = kv_all.shape[1] // (2 * HEAD)
    share = q_ref.shape[1] // (mine * HEAD)
    tile = q_ref.shape[0]
    step = pl.program_id(0)
    key_tiles = kv_all.shape[0] // KEY_TILE

    @pl.when(step == 0)
    def _():
        block_rows = kv_all.shape[0] // blocks
        load_keys(kv_refs, kv_all, sem, block_rows, key_columns(k_heads, k_first, mine))
        turn_blocks(kv_all, k_turned, 0, mine)
        dkv[...] = jnp.zeros_like(dkv)

    dq[...] = jnp.zeros_like(dq)
    for h in range(mine * share):
        g, j = h // share, h % share
        here = slice(h * HEAD, (h + 1) * HEAD)
        there = slice(j * tile, (j + 1) * tile)
        q_rows[g, there] = q_ref[:, here]
        q_turned[g, :, there] = jnp.transpose(q_ref[:, here])
        d_rows[g, there] = dout_ref[:, here]
        d_turned[g, :, there] = jnp.transpose(dout_ref[:, here])

    q_first = k_first * share

    def row_of(ref, g, first):
        cut = first + g * share
        return jnp.concatenate([ref[cut + j : cut + j + 1, :] for j in range(share)], axis=1)

    @pl.loop(0, key_tiles)
    def _(t):
        @pl.when(flags_ref[step * key_tiles + t] > 0)
        def _():
            rows = pl.ds(pl.multiple_of(t * KEY_TILE, KEY_TILE), KEY_TILE)
            bias = bias_ref[rows, :]
            bias = jnp.concatenate([bias] * share, axis=1)
            for first in range(0, mine, BACKWARD_HEADS):
                found = range(first, min(first + BACKWARD_HEADS, mine))
                scores = [
                    matmul(kv_all[rows, g * HEAD : (g + 1) * HEAD], q_turned[g]) for g in found
                ]
                dprobs = [
                    matmul(kv_all[rows, (mine + g) * HEAD : (mine + g + 1) * HEAD], d_turned[g])
                    for g in found
                ]
                probs = [
                    jnp.exp2(score * (SCALE * LOG2E) + bias - row_of(lse_ref, g, q_first))
                    for g, score in zip(found, scores)
                ]
                dscores = [
                    (prob * (dprob - row_of(delta_ref, g, q_first))).astype(BF16)
                    for g, prob, dprob in zip(found, probs, dprobs)
                ]
                dvs = [matmul(prob.astype(BF16), d_rows[g]) for g, prob in zip(found, probs)]
                dks = [matmul(dscore, q_rows[g]) for g, dscore in zip(found, dscores)]
                dqs = [
                    matmul(k_turned[g, :, rows], dscore) for g, dscore in zip(found, dscores)
                ]
                for k, g in enumerate(found):
                    dkv[rows, (mine + g) * HEAD : (mine + g + 1) * HEAD] += dvs[k]
                    dkv[rows, g * HEAD : (g + 1) * HEAD] += dks[k]
                    dq[g] += dqs[k]

    for h in range(mine * share):
        g, j = h // share, h % share
        dq_out[:, h * HEAD : (h + 1) * HEAD] = jnp.transpose(
            dq[g, :, j * tile : (j + 1) * tile] * SCALE
        )

    @pl.when(step == pl.num_programs(0) - 1)
    def _():
        half = kv_all.shape[0] // 2
        k_all = slice(0, mine * HEAD)
        v_all = slice(mine * HEAD, 2 * mine * HEAD)
        for out, first in ((keep_out, 0), (send_out, half)):
            out[:, k_all] = (dkv[first : first + half, k_all] * SCALE).astype(BF16)
            out[:, v_all] = dkv[first : first + half, v_all].astype(BF16)


def attend_back(
    flags, tile, queries, dout, bias, lse, delta, kvs, q_heads, k_heads, k_first, k_count
):
    rows = queries.shape[0]
    blocks = len(kvs)
    keys = sum(kv.shape[0] for kv in kvs)
    share = q_heads // k_heads
    q_width, kv_width = k_count * share * HEAD, 2 * k_count * HEAD
    column = k_first // k_count

    def at(width, column=0):
        return pl.BlockSpec((tile, width), lambda i, flags: (i, column))

    whole = pl.BlockSpec((keys // 2, kv_width), lambda i, flags: (0, 0))

    def by_lane(array):
        return pl.BlockSpec((array.shape[0], tile), lambda i, flags: (0, i))

    return pl.pallas_call(
        functools.partial(attend_back_kernel, k_heads, k_first, blocks),
        grid_spec=pltpu.PrefetchScalarGridSpec(
            num_scalar_prefetch=1,
            grid=(rows // tile,),
            in_specs=[
                at(q_width, column),
                at(q_width, column),
                pl.BlockSpec((None, keys, tile), lambda i, flags: (i, 0, 0)),
                by_lane(lse),
                by_lane(delta),
            ]
            + [pl.BlockSpec(memory_space=pl.ANY)] * blocks,
            out_specs=[at(q_width), whole, whole],
            scratch_shapes=[
                pltpu.VMEM((keys, kv_width), BF16),
                pltpu.VMEM((k_count, HEAD, keys), BF16),
                pltpu.VMEM((keys, kv_width), F32),
                pltpu.VMEM((k_count, share * tile, HEAD), BF16),
                pltpu.VMEM((k_count, HEAD, share * tile), BF16),
                pltpu.VMEM((k_count, share * tile, HEAD), BF16),
                pltpu.VMEM((k_count, HEAD, share * tile), BF16),
                pltpu.VMEM((k_count, HEAD, share * tile), F32),
                pltpu.SemaphoreType.DMA((blocks, 2)),
            ],
        ),
        out_shape=[
            shaped((rows, q_width), F32),
            shaped((keys // 2, kv_width), BF16),
            shaped((keys // 2, kv_width), BF16),
        ],
        compiler_params=params(),
        cost_estimate=cost(
            2 * rows * keys * q_width * 5, rows * keys * 4, rows * keys * q_width // HEAD
        ),
        name="attend_back",
    )(flags, queries, dout, bias, lse, delta, *kvs)


def per_device(
    sizes,
    tokens,
    seg_ids,
    positions,
    cotangent,
    norm_in,
    norm_mid,
    query_gain,
    key_gain,
    query_weight,
    key_matrix,
    value_matrix,
    head_weight,
    out_weight,
    gate_weight,
    up_weight,
    down_weight,
):
    n_shard, n_ctx, n_tp = sizes
    ring = Ring(n_shard, n_ctx)
    row_count, width = tokens.shape
    block = query_weight.shape[0]
    q_width = query_weight.shape[1]
    k_width = key_matrix.shape[1]
    q_heads, k_heads = q_width // HEAD, k_width // HEAD
    chunk = gate_weight.shape[1] // CHUNKS
    rows = row_count // n_tp
    tile = row_tile(rows)
    n_head = head_weight.shape[1]
    gain_size = query_gain.shape[0]

    here_ctx = lax.axis_index("ctx")
    here_tp = lax.axis_index("tp")
    here = lax.axis_index("shard") * n_ctx + here_ctx
    order = lax.dynamic_index_in_dim(jnp.asarray(ring.order), here, keepdims=False)

    def row_tiles(size):
        ids = np.arange(row_count // size)
        per = rows // size
        return (((here_tp + ids // per) % n_tp) * per + ids % per).astype(jnp.int32)

    tiles = row_tiles(tile)

    def padded(gain):
        return jnp.pad(gain, (0, block - gain_size))[:, None]

    send_a = jnp.concatenate(
        [
            query_weight,
            head_weight,
            jnp.zeros((block, GAINS - n_head), BF16),
            norm_in[:, None],
            norm_mid[:, None],
            padded(query_gain),
            padded(key_gain),
            jnp.zeros((block, LANES - GAINS - 4), BF16),
        ],
        axis=1,
    )

    def chunk_block(j, *others):
        cut = slice(j * chunk, (j + 1) * chunk)
        gate, up, down = gate_weight[:, cut], up_weight[:, cut], down_weight[cut]
        gate, up, down = lax.optimization_barrier((gate, up, down, *others))[:3]
        return jnp.concatenate([gate, up, down.T], axis=1)

    ring_a = Gather(ring, send_a)
    ring_b = Gather(ring, jnp.concatenate([key_matrix, value_matrix], axis=1))

    clock = Clock()
    tick, gate = clock.tick, clock.gate

    tick([], ring_a, ring_b)
    tok, cot, scale_in = enter(order, tiles, tile, tokens, cotangent)
    offset = here_ctx * row_count

    def own_rows(values):
        parts = [
            lax.dynamic_slice_in_dim(values, offset + ((here_tp + j) % n_tp) * rows, rows)
            for j in range(n_tp)
        ]
        return jnp.concatenate(parts)

    own_seg, own_pos = own_rows(seg_ids), own_rows(positions)
    block_order = sorted(range(n_ctx), key=lambda m: (m & 1, m))

    def key_rows(values):
        return jnp.concatenate(
            [
                lax.dynamic_slice_in_dim(values, (here_ctx ^ m) * row_count, row_count)
                for m in block_order
            ]
        )

    key_seg, key_pos = key_rows(seg_ids), key_rows(positions)
    tick([tok], ring_a, ring_b)
    half = HEAD // 2
    frequency = THETA ** (-(jnp.arange(half, dtype=F32) * 2.0) / HEAD)
    angles = own_pos.astype(F32)[:, None] * frequency[None, :]
    cos, sin = jnp.cos(angles), jnp.sin(angles)
    cos = jnp.concatenate([cos, cos], axis=1)
    sin = jnp.concatenate([-sin, sin], axis=1)
    ring_o = Gather(ring, hold(out_weight.T, cos))
    tick([cos, sin], ring_a, ring_b, ring_o)
    key_pos = gate(hold(key_pos, cos))
    q_tiles, key_tiles = row_count // ROW_TILE, key_seg.shape[0] // KEY_TILE
    q_seg, q_pos = (v.reshape(q_tiles, 1, ROW_TILE) for v in (own_seg, own_pos))
    k_seg, k_pos = key_seg[None, :, None], key_pos[None, :, None]
    allowed = ((k_seg == 0) | (k_seg == q_seg)) & (k_pos <= q_pos)
    bias = jnp.where(allowed, 0.0, MASKED).astype(F32)
    tick([bias], ring_a, ring_b, ring_o)
    flags = jnp.max(
        allowed.astype(jnp.int32).reshape(q_tiles, key_tiles, KEY_TILE, ROW_TILE), axis=(2, 3)
    ).reshape(-1)
    tick([flags], ring_a, ring_b, ring_o)
    tick([], ring_a, ring_b, ring_o)
    ring_c = [Gather(ring, chunk_block(0, ring_a.last))]
    tick([], ring_a, ring_b, ring_o)
    ring_c.append(Gather(ring, chunk_block(1, ring_a.last)))
    tick([ring_a.last], ring_o, ring_c[0], ring_c[1])

    wide, head = gather_gains(order, ring_a.pieces, q_width)
    normed, raw_a, raw_b, queries, kv, sg = project(
        row_tiles(rows),
        rows,
        gate(tok),
        scale_in,
        wide,
        head,
        cos,
        sin,
        ring_a.pieces,
        ring_b.pieces,
        q_heads,
        k_heads,
    )
    kvs = {0: kv}
    bit = n_ctx // 2
    while bit:
        for m in list(kvs):
            kvs[m | bit] = lax.ppermute(kvs[m], "ctx", [(i, i ^ bit) for i in range(n_ctx)])
        bit //= 2
    kvs = [kvs[m] for m in block_order]
    cot_turned = flip([gate(hold(cot, queries))], "flip_cot")
    tick([cot_turned], ring_o)
    ring_c.append(Gather(ring, chunk_block(2, cot_turned)))
    tick([kvs[-1]], *ring_c)
    att, gated, lse = attend(
        flags, ROW_TILE, gate(queries), bias, sg, kvs, q_heads, k_heads, 0, k_heads
    )
    tick([gated], ring_c[0])
    own, sent = spread([(gate(gated), ring_o.pieces, 0)], rows, "out_rows")
    arrived = tp_send(sent, rows, n_tp)
    tick([sent], *ring_c)
    tick([], *ring_c)
    middle, low = by_rows(
        middle_kernel, rows, tile, [gate(own), tok], wide, arrived, [F32, BF16], "middle"
    )
    normed_mid = tp_gather(low, n_tp)
    tick([low], *ring_c)
    tick([], *ring_c)

    def units(j):
        normed = [gate(normed_mid[0])] + normed_mid[1:]
        return ff_units(normed, cot, ring_c[j].pieces, 0, chunk)

    def weight_grads(j):
        hidden, dgate, dup = made[j]
        kept, sent = outer(
            [normed_turned, cot_turned], [gate(dgate), dup, hidden], [0, 0, 1], "unit_grads"
        )
        return clock.start(Reduce(ring, kept, sent))

    def mid_terms(j):
        return [
            (made[j][1], ring_c[j].pieces, 0),
            (made[j][2], ring_c[j].pieces, chunk),
        ]

    made = [units(0)]
    tick([made[0][0]], *ring_c)
    normed_turned = flip([gate(hold(normed_mid[0], made[0][0]))] + normed_mid[1:], "flip_mid")
    tick([normed_turned], *ring_c)
    sums_c = [weight_grads(0)]
    tick([sums_c[0].kept], *ring_c)
    normed_mid[0] = hold(normed_mid[0], sums_c[0].kept)
    made.append(units(1))
    tick([made[1][0]], ring_c[2], sums_c[0])
    (x, *rest), *others = mid_terms(0) + mid_terms(1)
    start = spread([(gate(x), *rest), *others], rows, "mid_start", split=False)[0]
    tick([start], ring_c[2], sums_c[0])
    normed_mid[0] = hold(normed_mid[0], start)
    made.append(units(2))
    tick([made[2][0]], sums_c[0])
    (x, *rest), *others = mid_terms(2)
    own, sent = spread([(gate(x), *rest), *others], rows, "mid_rows", start=start)
    arrived = tp_send(sent, rows, n_tp)
    tick([sent], sums_c[0])
    made[1] = [hold(part, sent) for part in made[1]]
    sums_c.append(weight_grads(1))
    tick([sums_c[1].kept], *sums_c)
    made[2] = [hold(part, sums_c[1].kept) for part in made[2]]
    sums_c.append(weight_grads(2))
    tick([sums_c[2].kept], *sums_c)
    dmid, low = by_rows(
        middle_back_kernel,
        rows,
        tile,
        [gate(hold(own, sums_c[2].kept)), cot, middle],
        wide,
        arrived,
        [F32, BF16],
        "middle_back",
    )
    dmid_low = tp_gather(low, n_tp)
    tick([low], *sums_c)
    terms = [(gate(hold(made[j][0], low)), ring_c[j].pieces, 2 * chunk) for j in range(CHUNKS)]
    mixed_own, mixed_sent = spread(terms, rows, "mixed_rows")
    tick([mixed_own], *sums_c)
    mixed_sent = hold(mixed_sent, dmid_low[-1])
    mixed_arrived = tp_send(mixed_sent, rows, n_tp)
    dmid_low[0] = hold(dmid_low[0], mixed_own)

    dout, delta, dlog = attended_back([gate(dmid_low[0])] + dmid_low[1:], ring_o.pieces, att, sg)
    tick([dout], *sums_c)
    dq, keep, sent = attend_back(
        flags, ROW_TILE, queries, gate(dout), bias, lse, delta, kvs, q_heads, k_heads, 0, k_heads
    )
    other = ring.swap(sent)
    extra = None
    for k in range(1, n_ctx // 2):
        piece = slice(k * row_count, (k + 1) * row_count)
        away = (keep[piece].astype(F32) + other[piece].astype(F32)).astype(BF16)
        m = block_order[k]
        came = lax.ppermute(away, "ctx", [(i, i ^ m) for i in range(n_ctx)])
        extra = came if extra is None else (extra.astype(F32) + came.astype(F32)).astype(BF16)
    dmid_low[0] = hold(dmid_low[0], away)
    dmid_turned = flip([gate(dmid_low[0])] + dmid_low[1:], "flip_dmid")
    tick([dmid_turned], *sums_c)
    sum_o = clock.start(
        Reduce(ring, *outer([dmid_turned], [gate(gated)], [0], "out_grad"))
    )
    normed_in_turned = flip([hold(normed, sum_o.kept)], "flip_in")
    output = by_rows(
        output_kernel,
        rows,
        tile,
        [hold(mixed_own, normed_in_turned), middle],
        None,
        mixed_arrived,
        [BF16],
        "output",
    )[0]
    output_parts = tp_gather(output, n_tp)
    tick([output], sum_o, *sums_c)
    d_a, d_b, gain_sums = heads_back(
        tiles,
        tile,
        [gate(hold(dq, output))],
        [[keep, other, extra]],
        [dlog],
        raw_a,
        raw_b,
        cos,
        sin,
        head,
        q_heads,
        k_heads,
    )
    tick([d_a], sum_o, *sums_c)
    sum_a = clock.start(
        Reduce(
            ring,
            *outer(
                [normed_in_turned],
                [gate(d_a)],
                [0],
                "query_grad",
                gains=(order, gain_sums),
                gained=q_width,
            ),
        )
    )
    tick([sum_a.kept], sum_o, *sums_c)
    sum_b = clock.start(
        Reduce(ring, *outer([normed_in_turned], [gate(hold(d_b, sum_a.kept))], [0], "key_grad"))
    )
    tick([sum_b.kept], sum_a, sum_o, *sums_c)
    own, sent = spread(
        [(gate(hold(d_a, sum_b.kept)), ring_a.pieces, 0), (d_b, ring_b.pieces, 0)], rows, "in_rows"
    )
    arrived = tp_send(sent, rows, n_tp)
    tick([sent], sum_a, sum_b, sum_o, *sums_c)
    tick([], sum_a, sum_b, sum_o)
    tick([], sum_a, sum_b, sum_o)
    low = by_rows(
        input_back_kernel,
        rows,
        tile,
        [gate(own), tok, scale_in, dmid],
        wide,
        arrived,
        [BF16],
        "input_back",
    )[0]
    parts = tp_gather(low, n_tp)
    tick([low], sum_a, sum_b, sum_o, *sums_c)
    output = leave(
        order,
        tiles,
        tile,
        [gate(hold(output_parts[0], low))] + output_parts[1:],
        BF16,
        "leave_output",
    )
    tick([output], sum_a, sum_b, sum_o)
    tick([], sum_a, sum_b, sum_o)
    parts[0] = gate(hold(parts[0], output))
    input_grad = leave(order, tiles, tile, parts, F32, "leave_grad")

    sums_c = [part.finish() for part in sums_c]
    sum_a, sum_b, sum_o = sum_a.finish(), sum_b.finish(), sum_o.finish()
    sum_gate = jnp.concatenate([part[:, :chunk] for part in sums_c], axis=1)
    sum_up = jnp.concatenate([part[:, chunk : 2 * chunk] for part in sums_c], axis=1)
    sum_down = jnp.concatenate([part[:, 2 * chunk :].T for part in sums_c], axis=0)
    mid_share = jnp.sum(sum_gate * gate_weight.astype(F32), axis=1) + jnp.sum(
        sum_up * up_weight.astype(F32), axis=1
    )
    in_share = (
        jnp.sum(sum_a[:, :q_width] * query_weight.astype(F32), axis=1)
        + jnp.sum(sum_b[:, :k_width] * key_matrix.astype(F32), axis=1)
        + jnp.sum(sum_b[:, k_width:] * value_matrix.astype(F32), axis=1)
        + jnp.sum(sum_a[:, q_width : q_width + n_head] * head_weight.astype(F32), axis=1)
    )
    small = jnp.stack(
        [
            in_share / norm_in.astype(F32),
            mid_share / norm_mid.astype(F32),
            sum_a[:, q_width + GAINS + 2],
            sum_a[:, q_width + GAINS + 3],
        ]
    )
    small = tp_total(small, n_tp)
    return (
        output,
        input_grad,
        small[0],
        small[1],
        small[2, :gain_size],
        small[3, :gain_size],
        sum_a[:, :q_width],
        sum_b[:, :k_width],
        sum_b[:, k_width:],
        sum_a[:, q_width : q_width + n_head],
        sum_o.T,
        sum_gate,
        sum_up,
        sum_down,
    )


def solution(mesh):
    sizes = (mesh.shape["shard"], mesh.shape["ctx"], mesh.shape["tp"])
    split = ("shard", "ctx")
    rows = P(split, None)
    vector = P(split)
    weight = P(split, "tp")
    turned = P("tp", split)
    return jax.shard_map(
        functools.partial(per_device, sizes),
        mesh=mesh,
        in_specs=(rows, P("shard"), P("shard"), rows)
        + (vector,) * 4
        + (weight,) * 4
        + (turned, weight, weight, turned),
        out_specs=(rows, rows) + (vector,) * 4 + (weight,) * 4 + (turned, weight, weight, turned),
        check_vma=False,
    )
```
